32 devices in a mesh: groups: 2 (over y), row: 16 (over z, x, core).
Axes of the slice: x: 2, y: 2, z: 4, core: 2. Of those that a mesh axis runs over, the one named last changes fastest.
Arguments:
- displacement: float32 [16, 3, 512, 512], P('groups', None, 'row'), parts along dimension 0, may hold values from -6 to 6
- loads: float32 [16, 3, 512, 512], P('groups', None, 'row'), parts along dimension 0, may hold values from -6 to 6
- section_stiffness: float32 [6, 512, 512], P('groups'), parts along dimension 0, may hold values from -0.125 to 2.5, as said below
- modulus: float32 [512, 1024], P('row', 'groups'), parts along dimension 1, may hold values from 0.3 to 3
- aggregate: int32 [6, 512, 512], P('groups', 'row'), parts along dimension 0, may hold values from 0 to 127
- basis_weight: float32 [6, 512, 512], P('groups', 'row'), parts along dimension 0, may hold values from 0.02 to 0.2
- diag_inverse: float32 [2048, 256], P('row', 'groups'), parts along dimension 1, may hold values from -0.031 to 0.3, as said below
- sub_factor: float32 [2048, 256], P('row', 'groups'), parts along dimension 1, may hold values from -1.35 to 1.35
Outputs:
- updated: float32 [16, 3, 512, 512], P('groups', None, 'row'), parts along dimension 0
- coarse_solution: float32 [2048, 16], P('row', 'groups'), parts along dimension 1
The draws below stay inside these ranges and needn't reach their ends.
There are 2 independent parts, one for each index of `groups`. The reference program is written for one: setup_inputs(seed, part) draws one part's arguments, and reference() takes and returns one part's arrays. A program takes and returns all parts, laid end to end along the dimension named above; each array names one. Nothing has to cross between parts.
Inputs may be any that keep to these rules, and one draw needn't show every extreme that they name: `section_stiffness`: each cross-section operator is symmetric, with diagonal entries in 1.5 to 2.5. `diag_inverse`: each block is lower triangular, with diagonal entries in 0.2 to 0.3.
All inputs are finite; a program needn't handle non-finite values.
Results may differ from the reference program's by a relative error of at most 0.00017.
Values sent between devices are 32-bit elements; how exact they have to be, the bound alone decides.
No kernel may reach another device: no remote copies, remote signals or barrier semaphores. Data moves between devices by JAX's collectives and lax.ppermute only.
A program may use at most 320 MiB of HBM per device.

```python
import math
import jax
import jax.numpy as jnp
from jax import lax

CASES = 8
SL = 32
W = 512
CPART = 128
NSPAN = 512
NCOARSE = 2048
N_ROW = 16


def draw_section_stiffness(key, part):
    diag_key = jax.random.fold_in(key, 11)
    off_key = jax.random.fold_in(key, 12)
    rows = lax.broadcasted_iota(jnp.int32, (3, W, W), 1)
    cols = lax.broadcasted_iota(jnp.int32, (3, W, W), 2)
    diag_vals = jax.random.uniform(diag_key, (3, W, W), jnp.float32, 1.5, 2.5)
    raw = jnp.clip(jax.random.normal(off_key, (3, W, W), jnp.float32), -4.0, 4.0)
    symmetric = (raw + jnp.swapaxes(raw, 1, 2)) * (0.35 / math.sqrt(W))
    symmetric = jnp.clip(symmetric, -0.125, 0.125)
    return jnp.where(rows == cols, diag_vals, symmetric)


def draw_diag_inverse(key, part):
    diag_key = jax.random.fold_in(key, 21)
    off_key = jax.random.fold_in(key, 22)
    rows = lax.broadcasted_iota(jnp.int32, (NCOARSE, CPART), 0) % CPART
    cols = lax.broadcasted_iota(jnp.int32, (NCOARSE, CPART), 1)
    diag_vals = jax.random.uniform(diag_key, (NCOARSE, CPART), jnp.float32, 0.2, 0.3)
    raw = jnp.clip(jax.random.normal(off_key, (NCOARSE, CPART), jnp.float32), -4.0, 4.0)
    lower = raw * (0.0875 / math.sqrt(CPART))
    return jnp.where(cols == rows, diag_vals, jnp.where(cols < rows, lower, 0.0))


def draw_sub_factor(key, part):
    sub_key = jax.random.fold_in(key, 31)
    spread = 3.8 / math.sqrt(CPART)
    raw = jnp.clip(jax.random.normal(sub_key, (NCOARSE, CPART), jnp.float32), -4.0, 4.0)
    return raw * spread


def plant(entries, stream_key, least, top_value):
    longest = entries.shape.index(max(entries.shape))
    spots = []
    for shift in (0, 1):
        where = [jax.random.randint(jax.random.fold_in(stream_key, axis), (), 0, length) for axis, length in enumerate(entries.shape)]
        where[longest] = (where[longest] + shift) % entries.shape[longest]
        spots.append(tuple(where))
    return entries.at[spots[0]].set(least).at[spots[1]].set(top_value)


def block_levels(own_key, extent, shards, smallest, high):
    gain, own = 1.0, jax.random.fold_in(own_key, 6)
    for axis_at, blocks in shards:
        draws = jnp.exp(jax.random.uniform(jax.random.fold_in(own, axis_at), (blocks,), jnp.float32, smallest / len(shards), high / len(shards)))
        gain = gain * jnp.repeat(draws, extent[axis_at] // blocks).reshape([-1 if axis == axis_at else 1 for axis in range(len(extent))])
    return gain


def scatter_about(stream_key, shape, width, bound, pieces=(), held_as=jnp.bfloat16):
    array = width * jax.random.normal(stream_key, shape, jnp.float32)
    if pieces:
        array = array * block_levels(stream_key, shape, pieces, -0.22, 0.18)
    return jnp.clip(array, -bound, bound).astype(held_as)


def setup_inputs(seed: int = 0, part: int = 0) -> dict:
    seeds = jax.random.split(jax.random.key(seed), 9)
    own_keys = jax.random.split(jax.random.fold_in(seeds[8], part), 9)
    displacement = scatter_about(own_keys[0], (CASES, 3, NSPAN, W), 1.0, 6.0, ((2, 16),), jnp.float32)
    loads = scatter_about(own_keys[1], (CASES, 3, NSPAN, W), 1.0, 6.0, ((2, 16),), jnp.float32)
    section_stiffness = draw_section_stiffness(jax.random.fold_in(jax.random.fold_in(seeds[8], part), 71), part)
    modulus = jnp.clip(jnp.exp(math.log(3.0) - 2.3025851 * jax.random.uniform(own_keys[3], (NSPAN, W), jnp.float32) ** block_levels(own_keys[3], (NSPAN, W), ((0, 16),), -0.2, 0.2)), 0.3, 3.0)
    aggregate = plant(jax.random.randint(own_keys[4], (3, NSPAN, W), 0, CPART), jax.random.fold_in(own_keys[4], 1), 0, CPART - 1).astype(jnp.int32)
    basis_weight = jnp.clip(jnp.exp(math.log(0.2) - 2.3025851 * jax.random.uniform(own_keys[5], (3, NSPAN, W), jnp.float32) ** block_levels(own_keys[5], (3, NSPAN, W), ((1, 16),), -0.2, 0.2)), 0.02, 0.2)
    diag_inverse = draw_diag_inverse(jax.random.fold_in(jax.random.fold_in(seeds[8], part), 71), part)
    sub_factor = draw_sub_factor(jax.random.fold_in(jax.random.fold_in(seeds[8], part), 71), part)
    return {"displacement": displacement, "loads": loads, "section_stiffness": section_stiffness, "modulus": modulus, "aggregate": aggregate, "basis_weight": basis_weight, "diag_inverse": diag_inverse, "sub_factor": sub_factor}


highest = lax.Precision.HIGHEST
span_weights = (1.5, -0.15, 1.0 / 90.0)


def matmul(left, right):
    return jnp.dot(left, right, precision=highest, preferred_element_type=jnp.float32)


def reference(displacement, loads, section_stiffness, modulus, aggregate, basis_weight, diag_inverse, sub_factor):
    num_cases, num_comps, span_total, section = displacement.shape
    padded = jnp.pad(displacement, ((0, 0), (0, 0), (3, 3), (0, 0)))
    span_sum = jnp.zeros_like(displacement)
    for offset in range(1, 4):
        layer_below = padded[:, :, 3 - offset:3 - offset + span_total]
        layer_above = padded[:, :, 3 + offset:3 + offset + span_total]
        span_sum = span_sum + span_weights[offset - 1] * (2.0 * displacement - layer_below - layer_above)
    across = jnp.einsum("casv,avw->casw", displacement, section_stiffness, precision=highest, preferred_element_type=jnp.float32)
    residual = loads - (modulus * span_sum + across)
    diag_total = modulus * (2.0 * sum(span_weights)) + jnp.diagonal(section_stiffness, axis1=1, axis2=2)[:, None, :]
    smoothed = residual / diag_total
    owner = jnp.arange(span_total, dtype=jnp.int32) // SL
    labels = (aggregate + CPART * owner[None, :, None]).astype(jnp.int32).reshape(-1)
    weighted = (basis_weight * residual).reshape(num_cases, -1).T
    coarse_rhs = jax.ops.segment_sum(weighted, labels, num_segments=NCOARSE)
    rhs_blocks = coarse_rhs.reshape(N_ROW, CPART, num_cases)
    inv_blocks = diag_inverse.reshape(N_ROW, CPART, CPART)
    sub_blocks = sub_factor.reshape(N_ROW, CPART, CPART)

    def forward_step(carry, inputs):
        inv_block, sub_block, rhs_block = inputs
        value = matmul(inv_block, rhs_block - matmul(sub_block, carry))
        return value, value

    start_value = jnp.zeros((CPART, num_cases), jnp.float32)
    last_value, forward_values = lax.scan(forward_step, start_value, (inv_blocks, sub_blocks, rhs_blocks))
    next_subs = jnp.roll(sub_blocks, -1, axis=0)

    def back_step(carry, inputs):
        inv_block, next_sub, value = inputs
        result = matmul(inv_block.T, value - matmul(next_sub.T, carry))
        return result, result

    first_value, back_values = lax.scan(back_step, start_value, (inv_blocks, next_subs, forward_values), reverse=True)
    coarse_solution = back_values.reshape(NCOARSE, num_cases)
    spread = jnp.take(coarse_solution.T, labels, axis=1).reshape(num_cases, num_comps, span_total, section)
    correction = basis_weight * spread
    updated = (displacement + smoothed) + correction
    return updated, coarse_solution
```

```python
import functools

import jax
import jax.numpy as jnp
from jax import lax
from jax.experimental import pallas as pl
from jax.experimental.pallas import tpu as pltpu
from jax.sharding import PartitionSpec as P

span_weights = (1.5, -0.15, 1.0 / 90.0)
bf16, f32 = jnp.bfloat16, jnp.float32
NN = (((1,), (0,)), ((), ()))
NT = (((1,), (1,)), ((), ()))
TN = (((0,), (0,)), ((), ()))


def split(value):
    high = value.astype(bf16)
    return high, (value - high.astype(f32)).astype(bf16)


def dot(left, right, dims):
    return lax.dot_general(left, right, dims, preferred_element_type=f32)


def dot3(left, right, dims):
    left_high, left_low = left
    right_high, right_low = right
    return dot(left_high, right_high, dims) + (
        dot(left_high, right_low, dims) + dot(left_low, right_high, dims)
    )


def residual_kernel(
    disp_ref, loads_ref, section_ref, modulus_ref, labels_ref, weight_ref, below_ref, above_ref,
    base_ref, rows_ref, padded, weighted,
):
    cases, _, layers, section = disp_ref.shape
    coarse = rows_ref.shape[1]
    tiles = section // 128
    stride = weighted.shape[0] // cases
    comp = pl.program_id(0)

    @pl.when(comp == 0)
    def _():
        rows_ref[...] = jnp.zeros_like(rows_ref)

    for tile in range(tiles):
        lanes = slice(tile * 128, (tile + 1) * 128)
        padded[:, tile, 8 : 8 + layers, :] = disp_ref[:, 0, :, lanes]
        padded[:, tile, 5:8, :] = below_ref[:, 0, :, lanes]
        padded[:, tile, 8 + layers : 11 + layers, :] = above_ref[:, 0, :, lanes]

    disp = split(disp_ref[:, 0].reshape(cases * layers, section))
    across = dot3(disp, split(section_ref[0]), NN).reshape(cases, layers, section)
    same = lax.broadcasted_iota(jnp.int32, (128, 128), 0) == lax.broadcasted_iota(
        jnp.int32, (128, 128), 1
    )
    for tile in range(tiles):
        lanes = slice(tile * 128, (tile + 1) * 128)
        block = section_ref[0, lanes, lanes]
        diagonal = jnp.sum(jnp.where(same, block, 0.0), axis=0, keepdims=True)
        modulus = modulus_ref[:, lanes]
        inverse = 1.0 / (modulus * (2.0 * sum(span_weights)) + diagonal)
        weight = weight_ref[0, :, lanes]
        for case in range(cases):
            own = padded[case, tile, 8 : 8 + layers, :]
            span_sum = jnp.zeros_like(own)
            for offset in range(1, 4):
                low = padded[case, tile, 8 - offset : 8 - offset + layers, :]
                high = padded[case, tile, 8 + offset : 8 + offset + layers, :]
                span_sum = span_sum + span_weights[offset - 1] * (2.0 * own - low - high)
            residual = loads_ref[case, 0, :, lanes] - (
                modulus * span_sum + across[case, :, lanes]
            )
            base_ref[case, 0, :, lanes] = own + residual * inverse
            start = case * stride + tile * layers
            weighted[start : start + layers, :] = weight * residual

    bins = lax.broadcasted_iota(jnp.int32, (coarse, 128), 0).astype(f32).astype(bf16)

    def restrict(group, total):
        first = pl.multiple_of(group * 8, 8)
        block = labels_ref[0, pl.ds(first, 8), :].astype(f32)
        for inner in range(8):
            layer = first + inner
            onehots, values = [], []
            for tile in range(tiles):
                lanes = slice(tile * 128, (tile + 1) * 128)
                label = jnp.broadcast_to(block[inner : inner + 1, lanes], (16, 128)).astype(bf16)
                label = jnp.concatenate([label] * (coarse // 16), axis=0)
                onehots.append(jnp.where(label == bins, bf16(1), bf16(0)))
                value = weighted[pl.ds(tile * layers + layer, cases, stride=stride), :]
                values.append(jnp.concatenate(split(value), axis=0))
            total = total + dot(
                jnp.concatenate(values, axis=1), jnp.concatenate(onehots, axis=1), NT
            )
        return total

    total = lax.fori_loop(0, layers // 8, restrict, jnp.zeros((2 * cases, coarse), f32))
    rows_ref[...] += total[:cases] + total[cases:]


def residual_call(disp, loads, section_stiffness, modulus, labels, weight, below, above, coarse):
    cases, comps, layers, section = disp.shape
    wide = pl.BlockSpec((cases, 1, layers, section), lambda a: (0, a, 0, 0))
    halo = pl.BlockSpec((cases, 1, 3, section), lambda a: (0, a, 0, 0))
    node = pl.BlockSpec((1, layers, section), lambda a: (a, 0, 0))
    tiles = section // 128
    return pl.pallas_call(
        residual_kernel,
        grid=(comps,),
        in_specs=[
            wide,
            wide,
            pl.BlockSpec((1, section, section), lambda a: (a, 0, 0)),
            pl.BlockSpec((layers, section), lambda a: (0, 0)),
            node,
            node,
            halo,
            halo,
        ],
        out_specs=[wide, pl.BlockSpec((cases, coarse), lambda a: (0, 0))],
        out_shape=[
            jax.ShapeDtypeStruct(disp.shape, f32),
            jax.ShapeDtypeStruct((cases, coarse), f32),
        ],
        scratch_shapes=[
            pltpu.VMEM((cases, tiles, layers + 16, 128), f32),
            pltpu.VMEM((cases * (tiles * layers + 8), 128), f32),
        ],
        compiler_params=pltpu.CompilerParams(vmem_limit_bytes=40 << 20),
        name="residual",
    )(disp, loads, section_stiffness, modulus, labels, weight, below, above)


def prolong_kernel(base_ref, labels_ref, weight_ref, solution_ref, updated_ref):
    cases, _, layers, section = base_ref.shape
    tables = [
        jnp.broadcast_to(solution_ref[case : case + 1, :], (layers, 128)) for case in range(cases)
    ]
    for tile in range(section // 128):
        lanes = slice(tile * 128, (tile + 1) * 128)
        label = labels_ref[0, :, lanes]
        weight = weight_ref[0, :, lanes]
        for case in range(cases):
            spread = jnp.take_along_axis(
                tables[case], label, axis=1, mode="promise_in_bounds"
            )
            updated_ref[case, 0, :, lanes] = base_ref[case, 0, :, lanes] + weight * spread


def prolong_call(base, labels, weight, solution_rows):
    cases, comps, layers, section = base.shape
    wide = pl.BlockSpec((cases, 1, layers, section), lambda a: (0, a, 0, 0))
    node = pl.BlockSpec((1, layers, section), lambda a: (a, 0, 0))
    return pl.pallas_call(
        prolong_kernel,
        grid=(comps,),
        in_specs=[wide, node, node, pl.BlockSpec(solution_rows.shape, lambda a: (0, 0))],
        out_specs=wide,
        out_shape=jax.ShapeDtypeStruct(base.shape, f32),
        compiler_params=pltpu.CompilerParams(vmem_limit_bytes=32 << 20),
        name="prolong",
    )(base, labels, weight, solution_rows)


def swap(value, axis, mask):
    count = lax.axis_size(axis)
    return lax.ppermute(value, axis, [(i, i ^ mask) for i in range(count)])


def matmul(left, right, dims):
    return lax.dot_general(
        left, right, dims, precision=lax.Precision.HIGHEST, preferred_element_type=f32
    )


def join_maps(first, second):
    phi_a, gram_a = first
    phi_b, gram_b = second
    return (
        matmul(phi_b, phi_a, NN),
        gram_a + matmul(phi_a, matmul(gram_b, phi_a, NN), TN),
    )


def join_shifts(maps_a, maps_b, first, second):
    ahead_a, back_a = first
    ahead_b, back_b = second
    phi_a, _ = maps_a
    phi_b, gram_b = maps_b
    return (
        matmul(ahead_a, phi_b, NT) + ahead_b,
        back_a + matmul(back_b - matmul(ahead_a, gram_b, NN), phi_a, NN),
    )


def pick(flag, one, other):
    return jax.tree.map(lambda a, b: jnp.where(flag, a, b), one, other)


def per_device(
    displacement, loads, section_stiffness, modulus, aggregate, basis_weight, diag_inverse, sub_factor
):
    layers = displacement.shape[2]
    coarse = diag_inverse.shape[1]
    count = lax.axis_size("row")
    mine = lax.axis_index("row")
    odd = (mine & 1) == 1

    first_layers = displacement[:, :, :3]
    last_layers = displacement[:, :, layers - 3 :]
    near = lax.ppermute(
        jnp.where(odd, first_layers, last_layers), "row", [(i, i ^ 1) for i in range(count)]
    )
    far = lax.ppermute(
        jnp.where(odd, last_layers, first_layers),
        "row",
        [(i, i + 1 if i & 1 else i - 1) for i in range(1, count - 1)],
    )
    below = jnp.where(odd, near, far)
    above = jnp.where(odd, far, near)

    step_map = -matmul(diag_inverse, sub_factor, NN)
    maps = (step_map, matmul(step_map, step_map, TN))
    strides = []
    while 4 << len(strides) < count:
        strides.append(1 << len(strides))
    levels = []
    for stride in strides:
        upper = (mine & stride) != 0
        others = jax.tree.map(lambda part: swap(part, "row", stride), maps)
        pair = pick(upper, others, maps), pick(upper, maps, others)
        levels.append((stride, upper, pair))
        maps = join_maps(*pair)
    width = 1 << len(strides)
    ways = count // width
    all_maps = [maps] + [
        jax.tree.map(lambda part, hop=hop: swap(part, "row", hop * width), maps)
        for hop in range(1, ways)
    ]

    base, rhs_rows = residual_call(
        displacement, loads, section_stiffness, modulus, aggregate, basis_weight, below, above, coarse
    )
    value = matmul(rhs_rows, diag_inverse, NT)
    shifts = (value, -matmul(value, step_map, NN))
    for position, (stride, upper, pair) in enumerate(levels):
        others = jax.tree.map(lambda part: swap(part, "row", stride), shifts)
        halves = pick(upper, others, shifts), pick(upper, shifts, others)
        levels[position] = (stride, upper, pair, halves)
        shifts = join_shifts(*pair, *halves)
    all_shifts = [shifts] + [
        jax.tree.map(lambda part, hop=hop: swap(part, "row", hop * width), shifts)
        for hop in range(1, ways)
    ]
    group = mine // width

    def in_order(parts):
        stacked = jax.tree.map(lambda *leaves: jnp.stack(leaves), *parts)
        return [
            jax.tree.map(lambda leaf, at=at: leaf[at ^ group], stacked) for at in range(ways)
        ]

    ordered_maps, ordered_shifts = in_order(all_maps), in_order(all_shifts)
    ahead = [jnp.zeros_like(value)]
    for (phi, _), (shift, _) in zip(ordered_maps[:-1], ordered_shifts[:-1]):
        ahead.append(matmul(ahead[-1], phi, NT) + shift)
    back = [jnp.zeros_like(value)]
    for at in range(ways - 1, 0, -1):
        phi, gram = ordered_maps[at]
        back.append(
            matmul(back[-1], phi, NN) - matmul(ahead[at], gram, NN) + ordered_shifts[at][1]
        )
    back = back[::-1]
    ahead, back = jnp.stack(ahead)[group], jnp.stack(back)[group]
    for stride, upper, (maps_a, maps_b), (shift_a, shift_b) in levels[::-1]:
        middle = matmul(ahead, maps_a[0], NT) + shift_a[0]
        inner = matmul(back, maps_b[0], NN) - matmul(middle, maps_b[1], NN) + shift_b[1]
        ahead = jnp.where(upper, middle, ahead)
        back = jnp.where(upper, back, inner)
    forward_value = matmul(ahead, step_map, NT) + value
    solution_rows = matmul(forward_value - back, diag_inverse, NN)
    updated = prolong_call(base, aggregate, basis_weight, solution_rows)
    return updated, solution_rows.T


def solution(mesh):
    placed = (
        P("groups", None, "row", None),
        P("groups", None, "row", None),
        P("groups", None, None),
        P("row", "groups"),
        P("groups", "row", None),
        P("groups", "row", None),
        P("row", "groups"),
        P("row", "groups"),
    )
    return jax.shard_map(
        per_device,
        mesh=mesh,
        in_specs=placed,
        out_specs=(P("groups", None, "row", None), P("row", "groups")),
        check_vma=False,
    )
```

```python
import functools

import jax
import jax.numpy as jnp
from jax import lax
from jax.experimental import pallas as pl
from jax.experimental.pallas import tpu as pltpu
from jax.sharding import PartitionSpec as P

span_weights = (1.5, -0.15, 1.0 / 90.0)
bf16, f32 = jnp.bfloat16, jnp.float32
NN = (((1,), (0,)), ((), ()))
NT = (((1,), (1,)), ((), ()))
TN = (((0,), (0,)), ((), ()))


def split(value):
    high = value.astype(bf16)
    return high, (value - high.astype(f32)).astype(bf16)


def dot(left, right, dims):
    return lax.dot_general(left, right, dims, preferred_element_type=f32)


def dot3(left, right, dims):
    left_high, left_low = left
    right_high, right_low = right
    return dot(left_high, right_high, dims) + (
        dot(left_high, right_low, dims) + dot(left_low, right_high, dims)
    )


def dot_rows(rows, weights, dims):
    high, low = split(rows)
    weight_high, weight_low = weights
    count = rows.shape[0]
    both = dot(jnp.concatenate([high, low], axis=0), weight_high, dims)
    return both[:count] + both[count:] + dot(high, weight_low, dims)


def residual_kernel(
    disp_ref, loads_ref, section_ref, modulus_ref, labels_ref, weight_ref, near_ref, far_ref,
    inverse_ref, base_ref, value_ref, padded, weighted, rows_ref,
):
    cases, _, layers, section = disp_ref.shape
    comps = pl.num_programs(0)
    coarse = rows_ref.shape[1]
    mine = lax.axis_index("row")
    odd = (mine & 1) == 1
    lowest, highest = mine == 0, mine == lax.axis_size("row") - 1
    tiles = section // 128
    stride = weighted.shape[0] // cases
    comp = pl.program_id(0)

    @pl.when(comp == 0)
    def _():
        rows_ref[...] = jnp.zeros_like(rows_ref)

    for tile in range(tiles):
        lanes = slice(tile * 128, (tile + 1) * 128)
        padded[:, tile, 8 : 8 + layers, :] = disp_ref[:, 0, :, lanes]
        for row in range(3):
            rows = pl.ds((tile * 3 + row) * cases * 3 + comp * cases, cases)
            near, far = near_ref[rows, :], far_ref[rows, :]
            below = jnp.where(lowest, 0.0, jnp.where(odd, near, far))
            above = jnp.where(highest, 0.0, jnp.where(odd, far, near))
            for case in range(cases):
                padded[case, tile, 5 + row : 6 + row, :] = below[case : case + 1]
                low = 8 + layers + row
                padded[case, tile, low : low + 1, :] = above[case : case + 1]

    disp = split(disp_ref[:, 0].reshape(cases * layers, section))
    across = dot3(disp, split(section_ref[0]), NN).reshape(cases, layers, section)
    same = lax.broadcasted_iota(jnp.int32, (128, 128), 0) == lax.broadcasted_iota(
        jnp.int32, (128, 128), 1
    )
    for tile in range(tiles):
        lanes = slice(tile * 128, (tile + 1) * 128)
        block = section_ref[0, lanes, lanes]
        diagonal = jnp.sum(jnp.where(same, block, 0.0), axis=0, keepdims=True)
        modulus = modulus_ref[:, lanes]
        inverse = 1.0 / (modulus * (2.0 * sum(span_weights)) + diagonal)
        weight = weight_ref[0, :, lanes]
        for case in range(cases):
            own = padded[case, tile, 8 : 8 + layers, :]
            span_sum = jnp.zeros_like(own)
            for offset in range(1, 4):
                low = padded[case, tile, 8 - offset : 8 - offset + layers, :]
                high = padded[case, tile, 8 + offset : 8 + offset + layers, :]
                span_sum = span_sum + span_weights[offset - 1] * (2.0 * own - low - high)
            residual = loads_ref[case, 0, :, lanes] - (
                modulus * span_sum + across[case, :, lanes]
            )
            base_ref[case, 0, :, lanes] = own + residual * inverse
            start = case * stride + tile * layers
            weighted[start : start + layers, :] = weight * residual

    bins = lax.broadcasted_iota(jnp.int32, (coarse, 128), 0).astype(f32).astype(bf16)

    def restrict(group, total):
        first = pl.multiple_of(group * 8, 8)
        block = labels_ref[0, pl.ds(first, 8), :].astype(f32)
        for inner in range(8):
            layer = first + inner
            onehots, values = [], []
            for tile in range(tiles):
                lanes = slice(tile * 128, (tile + 1) * 128)
                label = jnp.broadcast_to(block[inner : inner + 1, lanes], (16, 128)).astype(bf16)
                label = jnp.concatenate([label] * (coarse // 16), axis=0)
                onehots.append(jnp.where(label == bins, bf16(1), bf16(0)))
                value = weighted[pl.ds(tile * layers + layer, cases, stride=stride), :]
                values.append(jnp.concatenate(split(value), axis=0))
            total = total + dot(
                jnp.concatenate(values, axis=1), jnp.concatenate(onehots, axis=1), NT
            )
        return total

    total = lax.fori_loop(0, layers // 8, restrict, jnp.zeros((2 * cases, coarse), f32))
    rows_ref[...] += total[:cases] + total[cases:]

    @pl.when(comp == comps - 1)
    def _():
        value_ref[...] = dot_rows(rows_ref[...], split(inverse_ref[...]), NT)


def residual_call(disp, loads, section_stiffness, modulus, labels, weight, near, far, diag_inverse):
    cases, comps, layers, section = disp.shape
    wide = pl.BlockSpec((cases, 1, layers, section), lambda a: (0, a, 0, 0))
    coarse = diag_inverse.shape[0]
    halo = pl.BlockSpec((cases * comps * 3 * section // 128, 128), lambda a: (0, 0))
    node = pl.BlockSpec((1, layers, section), lambda a: (a, 0, 0))
    tiles = section // 128
    return pl.pallas_call(
        residual_kernel,
        grid=(comps,),
        in_specs=[
            wide,
            wide,
            pl.BlockSpec((1, section, section), lambda a: (a, 0, 0)),
            pl.BlockSpec((layers, section), lambda a: (0, 0)),
            node,
            node,
            halo,
            halo,
            pl.BlockSpec((coarse, coarse), lambda a: (0, 0)),
        ],
        out_specs=[wide, pl.BlockSpec((cases, coarse), lambda a: (0, 0))],
        out_shape=[
            jax.ShapeDtypeStruct(disp.shape, f32),
            jax.ShapeDtypeStruct((cases, coarse), f32),
        ],
        scratch_shapes=[
            pltpu.VMEM((cases, tiles, layers + 16, 128), f32),
            pltpu.VMEM((cases * (tiles * layers + 8), 128), f32),
            pltpu.VMEM((cases, coarse), f32),
        ],
        compiler_params=pltpu.CompilerParams(vmem_limit_bytes=18 << 20),
        name="residual",
    )(disp, loads, section_stiffness, modulus, labels, weight, near, far, diag_inverse)


def small(limit):
    return pltpu.CompilerParams(vmem_limit_bytes=limit << 20)


def start_kernel(
    inverse_hbm, sub_hbm, disp_hbm, step_ref, near_ref, far_ref, inverse, sub, first, last, sems
):
    cases, comps, rows, section = first.shape
    layers = disp_hbm.shape[2]
    copies = [
        pltpu.make_async_copy(inverse_hbm, inverse, sems.at[0]),
        pltpu.make_async_copy(sub_hbm, sub, sems.at[1]),
        pltpu.make_async_copy(disp_hbm.at[:, :, pl.ds(0, rows), :], first, sems.at[2]),
        pltpu.make_async_copy(disp_hbm.at[:, :, pl.ds(layers - rows, rows), :], last, sems.at[3]),
    ]
    for copy in copies:
        copy.start()
    odd = (lax.axis_index("row") & 1) == 1
    copies[0].wait()
    copies[1].wait()
    step_ref[...] = -dot3(split(inverse[...]), split(sub[...]), NN)
    copies[2].wait()
    copies[3].wait()
    for tile in range(section // 128):
        lanes = slice(tile * 128, (tile + 1) * 128)
        for row in range(3):
            for comp in range(comps):
                at = (tile * 3 + row) * cases * comps + comp * cases
                low = first[:, comp, row, lanes]
                high = last[:, comp, rows - 3 + row, lanes]
                near_ref[at : at + cases, :] = jnp.where(odd, low, high)
                far_ref[at : at + cases, :] = jnp.where(odd, high, low)


def start_call(diag_inverse, sub_factor, displacement):
    cases, comps, layers, section = displacement.shape
    packed = jax.ShapeDtypeStruct((cases * comps * 3 * section // 128, 128), f32)
    block = pltpu.VMEM((cases, comps, 8, section), f32)
    square = pltpu.VMEM(diag_inverse.shape, f32)
    return pl.pallas_call(
        start_kernel,
        in_specs=[pl.BlockSpec(memory_space=pltpu.HBM)] * 3,
        out_specs=[pl.BlockSpec(memory_space=pltpu.VMEM)] * 3,
        out_shape=[jax.ShapeDtypeStruct(diag_inverse.shape, f32), packed, packed],
        scratch_shapes=[square, square, block, block, pltpu.SemaphoreType.DMA((4,))],
        compiler_params=small(4),
        name="start",
    )(diag_inverse, sub_factor, displacement)


def pair_maps_kernel(own_ref, other_ref, maps_ref, mixed_ref):
    order = own_ref.shape[0]
    odd = (lax.axis_index("row") & 1) == 1
    own, other = own_ref[...], other_ref[...]
    first = jnp.where(odd, other, own)
    first_split, second_split = split(first), split(jnp.where(odd, own, other))
    phi = dot3(second_split, first_split, NN)
    phi_split = split(phi)
    maps_ref[:order, :] = phi
    maps_ref[order:, :] = dot3(first_split, first_split, TN) + dot3(phi_split, phi_split, TN)
    mixed_ref[...] = first + dot3(second_split, phi_split, TN)


def join_maps_kernel(stride, own_ref, other_ref, maps_ref, mixed_ref):
    order = own_ref.shape[1]
    upper = (lax.axis_index("row") & stride) != 0
    own, other = own_ref[...], other_ref[...]
    first, second = jnp.where(upper, other, own), jnp.where(upper, own, other)
    phi = split(first[:order])
    mixed = dot3(split(second[order:]), phi, NN)
    maps_ref[:order, :] = dot3(split(second[:order]), phi, NN)
    maps_ref[order:, :] = first[order:] + dot3(phi, split(mixed), TN)
    mixed_ref[...] = mixed


def maps_call(kernel, name, own, other):
    order = own.shape[1]
    return pl.pallas_call(
        kernel,
        out_shape=[
            jax.ShapeDtypeStruct((2 * order, order), f32),
            jax.ShapeDtypeStruct((order, order), f32),
        ],
        compiler_params=small(3),
        name=name,
    )(own, other)


def pair_shifts_kernel(own_ref, other_ref, own_step_ref, other_step_ref, maps_ref, mixed_ref, out_ref):
    cases, order = own_ref.shape
    odd = (lax.axis_index("row") & 1) == 1
    own, other = own_ref[...], other_ref[...]
    first, second = jnp.where(odd, other, own), jnp.where(odd, own, other)
    second_step = jnp.where(odd, own_step_ref[...], other_step_ref[...])
    out_ref[:cases, :] = dot_rows(first, split(second_step), NT) + second
    out_ref[cases:, :] = -(
        dot_rows(first, split(mixed_ref[...]), NN)
        + dot_rows(second, split(maps_ref[:order, :]), NN)
    )


def join_shifts_kernel(stride, own_ref, other_ref, own_maps_ref, other_maps_ref, mixed_ref, out_ref):
    order = mixed_ref.shape[0]
    cases = own_ref.shape[0] // 2
    upper = (lax.axis_index("row") & stride) != 0
    own, other = own_ref[...], other_ref[...]
    first, second = jnp.where(upper, other, own), jnp.where(upper, own, other)
    own_phi, other_phi = own_maps_ref[:order, :], other_maps_ref[:order, :]
    first_phi = jnp.where(upper, other_phi, own_phi)
    second_phi = jnp.where(upper, own_phi, other_phi)
    out_ref[:cases, :] = dot_rows(first[:cases], split(second_phi), NT) + second[:cases]
    out_ref[cases:, :] = (
        first[cases:]
        + dot_rows(second[cases:], split(first_phi), NN)
        - dot_rows(first[:cases], split(mixed_ref[...]), NN)
    )


def shifts_call(kernel, name, cases, *operands):
    return pl.pallas_call(
        kernel,
        out_shape=jax.ShapeDtypeStruct((2 * cases, operands[0].shape[1]), f32),
        compiler_params=small(3),
        name=name,
    )(*operands)


def finish_kernel(strides, width, ways, *refs):
    maps, refs = refs[:ways], refs[ways:]
    shifts, refs = refs[:ways], refs[ways:]
    levels = []
    for stride in strides:
        levels.append((stride, *refs[:4]))
        refs = refs[4:]
    (own_step_ref, other_step_ref, own_value_ref, other_value_ref, inverse_ref, base_hbm, labels_ref,
     weight_ref, updated_hbm, solution_hbm, all_maps, all_shifts, ahead_ref, back_ref, base, updated,
     solution, base_sems, out_sems) = refs
    cases, order = own_value_ref.shape
    comps, layers, section = labels_ref.shape
    mine = lax.axis_index("row")
    odd = (mine & 1) == 1
    group = mine // width

    base_copies = [
        pltpu.make_async_copy(base_hbm.at[:, comp], base.at[:, comp], base_sems.at[comp])
        for comp in range(comps)
    ]
    for copy in base_copies:
        copy.start()
    for hop in range(ways):
        all_maps[group ^ hop] = maps[hop][...]
        all_shifts[group ^ hop] = shifts[hop][...]

    ahead = all_shifts[0, :cases]
    ahead_ref[0] = jnp.zeros_like(ahead)
    ahead_ref[1] = ahead
    for at in range(1, ways - 1):
        ahead = dot_rows(ahead, split(all_maps[at, :order]), NT) + all_shifts[at, :cases]
        ahead_ref[at + 1] = ahead
    back = jnp.zeros_like(ahead)
    back_ref[ways - 1] = back
    for at in range(ways - 1, 0, -1):
        own = all_shifts[at, cases:] - dot_rows(ahead_ref[at], split(all_maps[at, order:]), NN)
        last = at == ways - 1
        back = own if last else own + dot_rows(back, split(all_maps[at, :order]), NN)
        back_ref[at - 1] = back
    ahead, back = ahead_ref[group], back_ref[group]

    for stride, own_maps, other_maps, own_shifts, other_shifts in levels[::-1]:
        upper = (mine & stride) != 0
        first_phi = jnp.where(upper, other_maps[:order, :], own_maps[:order, :])
        second_maps = jnp.where(upper, own_maps[...], other_maps[...])
        own, other = own_shifts[...], other_shifts[...]
        first_shift = jnp.where(upper, other[:cases], own[:cases])
        second_shift = jnp.where(upper, own[cases:], other[cases:])
        middle = dot_rows(ahead, split(first_phi), NT) + first_shift
        inner = (
            dot_rows(back, split(second_maps[:order]), NN)
            - dot_rows(middle, split(second_maps[order:]), NN)
            + second_shift
        )
        ahead = jnp.where(upper, middle, ahead)
        back = jnp.where(upper, back, inner)

    own_step, other_step = own_step_ref[...], other_step_ref[...]
    own_value, other_value = own_value_ref[...], other_value_ref[...]
    first_step = split(jnp.where(odd, other_step, own_step))
    second_step = split(jnp.where(odd, own_step, other_step))
    first = dot_rows(ahead, first_step, NT) + jnp.where(odd, other_value, own_value)
    second = dot_rows(first, second_step, NT) + jnp.where(odd, own_value, other_value)
    inner = dot_rows(back - second, second_step, NN)
    solved = dot_rows(
        jnp.where(odd, second - back, first - inner), split(inverse_ref[...]), NN
    )
    solution[...] = solved.T
    out_copies = [pltpu.make_async_copy(solution, solution_hbm, out_sems.at[comps])]
    out_copies[0].start()

    for comp in range(comps):
        base_copies[comp].wait()
        for tile in range(section // 128):
            lanes = slice(tile * 128, (tile + 1) * 128)
            label = labels_ref[comp, :, lanes]
            weight = weight_ref[comp, :, lanes]
            for case in range(cases):
                table = jnp.broadcast_to(solved[case : case + 1, :], (layers, 128))
                spread = jnp.take_along_axis(table, label, axis=1, mode="promise_in_bounds")
                updated[case, comp, :, lanes] = base[case, comp, :, lanes] + weight * spread
        copy = pltpu.make_async_copy(
            updated.at[:, comp], updated_hbm.at[:, comp], out_sems.at[comp]
        )
        copy.start()
        out_copies.append(copy)
    for copy in out_copies:
        copy.wait()


def finish_call(strides, width, maps, shifts, levels, leaf, base, labels, weight):
    cases, comps, layers, section = base.shape
    order = maps[0].shape[1]
    ways = len(maps)
    hbm, local = pl.BlockSpec(memory_space=pltpu.HBM), pl.BlockSpec(memory_space=pltpu.VMEM)
    before = (*maps, *shifts, *levels, *leaf)
    return pl.pallas_call(
        functools.partial(finish_kernel, strides, width, ways),
        in_specs=[local] * len(before) + [hbm, local, local],
        out_specs=[hbm, hbm],
        out_shape=[
            jax.ShapeDtypeStruct(base.shape, f32),
            jax.ShapeDtypeStruct((order, cases), f32),
        ],
        scratch_shapes=[
            pltpu.VMEM((ways, 2 * order, order), f32),
            pltpu.VMEM((ways, 2 * cases, order), f32),
            pltpu.VMEM((ways, cases, order), f32),
            pltpu.VMEM((ways, cases, order), f32),
            pltpu.VMEM(base.shape, f32),
            pltpu.VMEM(base.shape, f32),
            pltpu.VMEM((order, cases), f32),
            pltpu.SemaphoreType.DMA((comps,)),
            pltpu.SemaphoreType.DMA((comps + 1,)),
        ],
        compiler_params=small(10),
        name="finish",
    )(*before, base, labels, weight)


def per_device(
    displacement, loads, section_stiffness, modulus, aggregate, basis_weight, diag_inverse, sub_factor
):
    cases = displacement.shape[0]
    count = lax.axis_size("row")
    ways = 4
    width = count // ways

    def swap(value, mask):
        return lax.ppermute(value, "row", [(i, i ^ mask) for i in range(count)])

    step, near, far = start_call(diag_inverse, sub_factor, displacement)
    other_step = swap(step, 1)
    near = swap(near, 1)
    far = lax.ppermute(
        far, "row", [(i, i + 1 if i & 1 else i - 1) for i in range(1, count - 1)]
    )
    maps, mixed = maps_call(pair_maps_kernel, "pair_maps", step, other_step)
    pair_operands = (step, other_step, maps, mixed)
    strides, joins = [], []
    stride = 2
    while stride < width:
        other_maps = swap(maps, stride)
        joined, mixed = maps_call(
            functools.partial(join_maps_kernel, stride), "join_maps", maps, other_maps
        )
        strides.append(stride)
        joins.append((maps, other_maps, mixed))
        maps = joined
        stride *= 2
    all_maps = [maps] + [swap(maps, hop * width) for hop in range(1, ways)]

    base, value = residual_call(
        displacement, loads, section_stiffness, modulus, aggregate, basis_weight, near, far,
        diag_inverse,
    )
    other_value = swap(value, 1)
    shifts = shifts_call(pair_shifts_kernel, "pair_shifts", cases, value, other_value, *pair_operands)
    levels = []
    for stride, (own_maps, other_maps, mixed) in zip(strides, joins):
        other_shifts = swap(shifts, stride)
        levels += [own_maps, other_maps, shifts, other_shifts]
        shifts = shifts_call(
            functools.partial(join_shifts_kernel, stride), "join_shifts", cases,
            shifts, other_shifts, own_maps, other_maps, mixed,
        )
    all_shifts = [shifts] + [swap(shifts, hop * width) for hop in range(1, ways)]
    leaf = (step, other_step, value, other_value, diag_inverse)
    return finish_call(
        tuple(strides), width, all_maps, all_shifts, levels, leaf, base, aggregate, basis_weight
    )


def solution(mesh):
    placed = (
        P("groups", None, "row", None),
        P("groups", None, "row", None),
        P("groups", None, None),
        P("row", "groups"),
        P("groups", "row", None),
        P("groups", "row", None),
        P("row", "groups"),
        P("row", "groups"),
    )
    return jax.shard_map(
        per_device,
        mesh=mesh,
        in_specs=placed,
        out_specs=(P("groups", None, "row", None), P("row", "groups")),
        check_vma=False,
    )
```

```python
import functools

import jax
import jax.numpy as jnp
from jax import lax
from jax.experimental import pallas as pl
from jax.experimental.pallas import tpu as pltpu
from jax.sharding import PartitionSpec as P

span_weights = (1.5, -0.15, 1.0 / 90.0)
bf16, f32 = jnp.bfloat16, jnp.float32
NN = (((1,), (0,)), ((), ()))
NT = (((1,), (1,)), ((), ()))
TN = (((0,), (0,)), ((), ()))


def split(value):
    high = value.astype(bf16)
    return high, (value - high.astype(f32)).astype(bf16)


def dot(left, right, dims):
    return lax.dot_general(left, right, dims, preferred_element_type=f32)


def dot3(left, right, dims):
    left_high, left_low = left
    right_high, right_low = right
    return dot(left_high, right_high, dims) + (
        dot(left_high, right_low, dims) + dot(left_low, right_high, dims)
    )


def dot_rows(rows, weights, dims):
    high, low = split(rows)
    weight_high, weight_low = weights
    count = rows.shape[0]
    both = dot(jnp.concatenate([high, low], axis=0), weight_high, dims)
    return both[:count] + both[count:] + dot(high, weight_low, dims)


def node_rows(edge, layers):
    return (0, layers - 8) if edge else tuple(range(8, layers - 8, 8))


def residual_part(
    edge, disp_ref, loads_ref, modulus_ref, labels_ref, weight_ref, across_ref, diagonal_of, padded,
    weighted, base_ref, comp, total,
):
    cases, comps, layers, section = disp_ref.shape
    tiles = section // 128
    groups = node_rows(edge, layers)
    depth = 8 * len(groups)
    stride = weighted.shape[1] // cases
    fine = total.shape[1]
    parts = total.shape[0] // (2 * cases)
    bins = lax.broadcasted_iota(jnp.int32, (fine, 128), 0).astype(f32).astype(bf16)
    for at, first in enumerate(groups):
        rows = slice(first, first + 8)
        out = slice(at * 8, at * 8 + 8)
        for tile in range(tiles):
            lanes = slice(tile * 128, (tile + 1) * 128)
            modulus = modulus_ref[rows, lanes]
            diagonal = diagonal_of(comp, lanes)
            inverse = 1.0 / (modulus * (2.0 * sum(span_weights)) + diagonal)
            weight = weight_ref[comp, rows, lanes]
            for case in range(cases):
                own = padded[comp, case, tile, 8 + first : 16 + first, :]
                span_sum = (2.0 * sum(span_weights)) * own
                for offset in range(1, 4):
                    low = padded[comp, case, tile, 8 + first - offset : 16 + first - offset, :]
                    high = padded[comp, case, tile, 8 + first + offset : 16 + first + offset, :]
                    span_sum = span_sum - span_weights[offset - 1] * (low + high)
                residual = loads_ref[case, comp, rows, lanes] - (
                    modulus * span_sum + across_ref[comp, case, out, lanes]
                )
                base_ref[case, comp, out, lanes] = own + residual * inverse
                start = case * stride + tile * depth + at * 8
                weighted[comp, start : start + 8, :] = weight * residual

    def restrict(group, total):
        at = pl.multiple_of(group * 8, 8)
        first = pl.multiple_of(groups[0] + group * (groups[1] - groups[0]), 8)
        block = labels_ref[comp, pl.ds(first, 8), :]
        big = lax.shift_right_logical(block, fine.bit_length() - 1).astype(f32)
        little = (block & (fine - 1)).astype(f32)
        for inner in range(8):
            onehots, values = [], []
            for tile in range(tiles):
                lanes = slice(tile * 128, (tile + 1) * 128)
                low = jnp.broadcast_to(little[inner : inner + 1, lanes], (16, 128)).astype(bf16)
                low = jnp.concatenate([low] * (fine // 16), axis=0)
                onehots.append(jnp.where(low == bins, bf16(1), bf16(0)))
                high = jnp.broadcast_to(big[inner : inner + 1, lanes], (16, 128)).astype(bf16)
                value = weighted[comp, pl.ds(tile * depth + at + inner, cases, stride=stride), :]
                value = jnp.concatenate(split(value), axis=0)
                values.append(
                    jnp.concatenate(
                        [jnp.where(high == bf16(part), value, bf16(0)) for part in range(parts)],
                        axis=0,
                    )
                )
            total = total + dot(
                jnp.concatenate(values, axis=1), jnp.concatenate(onehots, axis=1), NT
            )
        return total

    return lax.fori_loop(0, len(groups), restrict, total)


def inner_kernel(
    disp_ref, loads_ref, section_ref, modulus_ref, labels_ref, weight_ref,
    base_ref, outer_ref, diagonal_ref, total_ref, padded, weighted, across_ref,
):
    cases, comps, layers, section = disp_ref.shape
    tiles = section // 128
    same = lax.broadcasted_iota(jnp.int32, (128, 128), 0) == lax.broadcasted_iota(
        jnp.int32, (128, 128), 1
    )
    total = jnp.zeros(total_ref.shape, f32)
    for comp in range(comps):
        for tile in range(tiles):
            lanes = slice(tile * 128, (tile + 1) * 128)
            padded[comp, :, tile, 8 : 8 + layers, :] = disp_ref[:, comp, :, lanes]
        high, low = split(disp_ref[:, comp].reshape(cases * layers, section))
        section_high, section_low = split(section_ref[comp])
        across = dot(
            jnp.concatenate([high, high, low], axis=1),
            jnp.concatenate([section_high, section_low, section_high], axis=0),
            NN,
        ).reshape(cases, layers, section)
        across_ref[comp] = across[:, 8 : layers - 8]
        outer_ref[comp, :, :8] = across[:, :8]
        outer_ref[comp, :, 8:] = across[:, layers - 8 :]
        diagonals = []
        for tile in range(tiles):
            lanes = slice(tile * 128, (tile + 1) * 128)
            block = section_ref[comp, lanes, lanes]
            diagonals.append(jnp.sum(jnp.where(same, block, 0.0), axis=0, keepdims=True))
            diagonal_ref[comp, :, lanes] = jnp.broadcast_to(diagonals[-1], (8, 128))
        total = residual_part(
            False, disp_ref, loads_ref, modulus_ref, labels_ref, weight_ref, across_ref,
            lambda _, lanes: diagonals[lanes.start // 128], padded, weighted, base_ref, comp, total,
        )
    total_ref[...] = total


def outer_kernel(
    disp_ref, loads_ref, modulus_ref, labels_ref, weight_ref, inverse_ref, near_ref, far_ref,
    across_ref, diagonal_ref, inner_total_ref, base_ref, value_ref, padded, weighted,
):
    cases, comps, layers, section = disp_ref.shape
    mine = lax.axis_index("row")
    odd = (mine & 1) == 1
    lowest, highest = mine == 0, mine == lax.axis_size("row") - 1
    tiles = section // 128
    total = inner_total_ref[...]
    for comp in range(comps):
        for tile in range(tiles):
            lanes = slice(tile * 128, (tile + 1) * 128)
            padded[comp, :, tile, 8:24, :] = disp_ref[:, comp, :16, lanes]
            padded[comp, :, tile, layers - 8 : layers + 8, :] = disp_ref[
                :, comp, layers - 16 :, lanes
            ]
            for row in range(3):
                at = (tile * 3 + row) * cases * comps + comp * cases
                near, far = near_ref[at : at + cases, :], far_ref[at : at + cases, :]
                below = jnp.where(lowest, 0.0, jnp.where(odd, near, far))
                above = jnp.where(highest, 0.0, jnp.where(odd, far, near))
                for case in range(cases):
                    padded[comp, case, tile, 5 + row : 6 + row, :] = below[case : case + 1]
                    low = 8 + layers + row
                    padded[comp, case, tile, low : low + 1, :] = above[case : case + 1]
        total = residual_part(
            True, disp_ref, loads_ref, modulus_ref, labels_ref, weight_ref, across_ref,
            lambda comp, lanes: diagonal_ref[comp, :, lanes], padded, weighted, base_ref, comp,
            total,
        )
    sums = []
    for at in range(0, total.shape[0], 2 * cases):
        sums.append(total[at : at + cases] + total[at + cases : at + 2 * cases])
    value_ref[...] = dot_rows(jnp.concatenate(sums, axis=1), split(inverse_ref[...]), NT)


def residual_call(kernel, edge, out_shape, scratch_shapes, *operands):
    cases, comps, layers, section = operands[0].shape
    tiles = section // 128
    depth = 8 * len(node_rows(edge, layers))
    local = pl.BlockSpec(memory_space=pltpu.VMEM)
    return pl.pallas_call(
        kernel,
        in_specs=[local] * len(operands),
        out_specs=[local] * len(out_shape),
        out_shape=[jax.ShapeDtypeStruct(shape, f32) for shape in out_shape],
        scratch_shapes=[
            pltpu.VMEM((comps, cases, tiles, layers + 16, 128), f32),
            pltpu.VMEM((comps, cases * (tiles * depth + 8), 128), f32),
            *scratch_shapes,
        ],
        compiler_params=pltpu.CompilerParams(vmem_limit_bytes=14 << 20),
        cost_estimate=pl.CostEstimate(
            flops=3 * cases * comps * layers * section * section,
            bytes_accessed=8 * operands[0].size,
            transcendentals=0,
        ),
        name="outer_residual" if edge else "inner_residual",
    )(*operands)


def small(limit):
    return pltpu.CompilerParams(vmem_limit_bytes=limit << 20)


def in_hbm(*values):
    return [pltpu.with_memory_space_constraint(value, pltpu.HBM) for value in values]


def start_kernel(
    inverse_hbm, sub_hbm, disp_hbm, step_ref, near_ref, far_ref, inverse, sub, first, last, sems
):
    cases, comps, rows, section = first.shape
    layers = disp_hbm.shape[2]
    copies = [
        pltpu.make_async_copy(inverse_hbm, inverse, sems.at[0]),
        pltpu.make_async_copy(sub_hbm, sub, sems.at[1]),
        pltpu.make_async_copy(disp_hbm.at[:, :, pl.ds(0, rows), :], first, sems.at[2]),
        pltpu.make_async_copy(disp_hbm.at[:, :, pl.ds(layers - rows, rows), :], last, sems.at[3]),
    ]
    for copy in copies:
        copy.start()
    odd = (lax.axis_index("row") & 1) == 1
    copies[0].wait()
    copies[1].wait()
    step_ref[...] = -dot3(split(inverse[...]), split(sub[...]), NN)
    copies[2].wait()
    copies[3].wait()
    for tile in range(section // 128):
        lanes = slice(tile * 128, (tile + 1) * 128)
        for row in range(3):
            for comp in range(comps):
                at = (tile * 3 + row) * cases * comps + comp * cases
                low = first[:, comp, row, lanes]
                high = last[:, comp, rows - 3 + row, lanes]
                near_ref[at : at + cases, :] = jnp.where(odd, low, high)
                far_ref[at : at + cases, :] = jnp.where(odd, high, low)


def start_call(diag_inverse, sub_factor, displacement):
    cases, comps, layers, section = displacement.shape
    packed = jax.ShapeDtypeStruct((cases * comps * 3 * section // 128, 128), f32)
    block = pltpu.VMEM((cases, comps, 8, section), f32)
    square = pltpu.VMEM(diag_inverse.shape, f32)
    return pl.pallas_call(
        start_kernel,
        in_specs=[pl.BlockSpec(memory_space=pltpu.HBM)] * 3,
        out_specs=[pl.BlockSpec(memory_space=pltpu.VMEM)] * 3,
        out_shape=[jax.ShapeDtypeStruct(diag_inverse.shape, f32), packed, packed],
        scratch_shapes=[square, square, block, block, pltpu.SemaphoreType.DMA((4,))],
        compiler_params=small(4),
        cost_estimate=pl.CostEstimate(flops=10**10, bytes_accessed=10**6, transcendentals=0),
        name="start",
    )(*in_hbm(diag_inverse, sub_factor, displacement))


def pair_maps_kernel(own_ref, other_ref, maps_ref, mixed_ref):
    order = own_ref.shape[0]
    odd = (lax.axis_index("row") & 1) == 1
    own, other = own_ref[...], other_ref[...]
    first = jnp.where(odd, other, own)
    first_split, second_split = split(first), split(jnp.where(odd, own, other))
    phi = dot3(second_split, first_split, NN)
    phi_split = split(phi)
    gram = dot3(first_split, first_split, TN) + dot3(phi_split, phi_split, TN)
    maps_ref[:order, :] = phi
    maps_ref[order:, :] = gram
    mixed_ref[...] = first + dot3(second_split, phi_split, TN)


def join_maps_kernel(stride, own_ref, other_ref, maps_ref, mixed_ref, half_ref):
    order = own_ref.shape[1]
    upper = (lax.axis_index("row") & stride) != 0
    own, other = own_ref[...], other_ref[...]
    first, second = jnp.where(upper, other, own), jnp.where(upper, own, other)
    first_phi = split(first[:order])
    mixed = dot3(split(second[order:]), first_phi, NN)
    phi = dot3(split(second[:order]), first_phi, NN)
    gram = first[order:] + dot3(first_phi, split(mixed), TN)
    maps_ref[:order, :] = phi
    maps_ref[order:, :] = gram
    mixed_ref[...] = mixed
    odd = (lax.axis_index("row") & 1) == 1
    half_ref[...] = jnp.where(odd, gram, phi)


def maps_call(kernel, name, extra, own, other):
    order = own.shape[1]
    return pl.pallas_call(
        kernel,
        out_shape=[
            jax.ShapeDtypeStruct((2 * order, order), f32),
        ]
        + [jax.ShapeDtypeStruct((order, order), f32)] * extra,
        compiler_params=small(3),
        cost_estimate=pl.CostEstimate(flops=10**10, bytes_accessed=10**6, transcendentals=0),
        name=name,
    )(own, other)


def pair_shifts_kernel(own_ref, other_ref, own_step_ref, other_step_ref, maps_ref, mixed_ref, out_ref):
    cases, order = own_ref.shape
    odd = (lax.axis_index("row") & 1) == 1
    own, other = own_ref[...], other_ref[...]
    first, second = jnp.where(odd, other, own), jnp.where(odd, own, other)
    second_step = jnp.where(odd, own_step_ref[...], other_step_ref[...])
    out_ref[:cases, :] = dot_rows(first, split(second_step), NT) + second
    out_ref[cases:, :] = -(
        dot_rows(first, split(mixed_ref[...]), NN)
        + dot_rows(second, split(maps_ref[:order, :]), NN)
    )


def join_shifts_kernel(stride, own_ref, other_ref, own_maps_ref, other_maps_ref, mixed_ref, out_ref):
    order = mixed_ref.shape[0]
    cases = own_ref.shape[0] // 2
    upper = (lax.axis_index("row") & stride) != 0
    own, other = own_ref[...], other_ref[...]
    first, second = jnp.where(upper, other, own), jnp.where(upper, own, other)
    own_phi, other_phi = own_maps_ref[:order, :], other_maps_ref[:order, :]
    first_phi = jnp.where(upper, other_phi, own_phi)
    second_phi = jnp.where(upper, own_phi, other_phi)
    out_ref[:cases, :] = dot_rows(first[:cases], split(second_phi), NT) + second[:cases]
    out_ref[cases:, :] = (
        first[cases:]
        + dot_rows(second[cases:], split(first_phi), NN)
        - dot_rows(first[:cases], split(mixed_ref[...]), NN)
    )


def shifts_call(kernel, name, cases, *operands):
    return pl.pallas_call(
        kernel,
        out_shape=jax.ShapeDtypeStruct((2 * cases, operands[0].shape[1]), f32),
        compiler_params=small(3),
        name=name,
    )(*operands)


def finish_kernel(strides, width, ways, *refs):
    own_maps_ref, halves, refs = refs[0], refs[1 : 2 * ways - 1], refs[2 * ways - 1 :]
    shifts, refs = refs[:ways], refs[ways:]
    levels = []
    for stride in strides:
        levels.append((stride, *refs[:4]))
        refs = refs[4:]
    (own_step_ref, other_step_ref, own_value_ref, other_value_ref, inverse_ref, inner_base, outer_base,
     labels_ref,
     weight_ref, updated_hbm, solution_hbm, all_maps, all_shifts, ahead_ref, back_ref, updated,
     solution, out_sems) = refs
    cases, order = own_value_ref.shape
    comps, layers, section = labels_ref.shape
    mine = lax.axis_index("row")
    odd = (mine & 1) == 1
    group = mine // width

    all_maps[group] = own_maps_ref[...]
    for hop in range(1, ways):
        got, swapped = halves[2 * hop - 2][...], halves[2 * hop - 1][...]
        all_maps[group ^ hop, :order] = jnp.where(odd, swapped, got)
        all_maps[group ^ hop, order:] = jnp.where(odd, got, swapped)
    for hop in range(ways):
        all_shifts[group ^ hop] = shifts[hop][...]

    ahead = all_shifts[0, :cases]
    ahead_ref[0] = jnp.zeros_like(ahead)
    ahead_ref[1] = ahead
    for at in range(1, ways - 1):
        ahead = dot_rows(ahead, split(all_maps[at, :order]), NT) + all_shifts[at, :cases]
        ahead_ref[at + 1] = ahead
    back = jnp.zeros_like(ahead)
    back_ref[ways - 1] = back
    for at in range(ways - 1, 0, -1):
        own = all_shifts[at, cases:] - dot_rows(ahead_ref[at], split(all_maps[at, order:]), NN)
        last = at == ways - 1
        back = own if last else own + dot_rows(back, split(all_maps[at, :order]), NN)
        back_ref[at - 1] = back
    ahead, back = ahead_ref[group], back_ref[group]

    for stride, own_maps, other_maps, own_shifts, other_shifts in levels[::-1]:
        upper = (mine & stride) != 0
        first_phi = jnp.where(upper, other_maps[:order, :], own_maps[:order, :])
        second_maps = jnp.where(upper, own_maps[...], other_maps[...])
        own, other = own_shifts[...], other_shifts[...]
        first_shift = jnp.where(upper, other[:cases], own[:cases])
        second_shift = jnp.where(upper, own[cases:], other[cases:])
        middle = dot_rows(ahead, split(first_phi), NT) + first_shift
        inner = (
            dot_rows(back, split(second_maps[:order]), NN)
            - dot_rows(middle, split(second_maps[order:]), NN)
            + second_shift
        )
        ahead = jnp.where(upper, middle, ahead)
        back = jnp.where(upper, back, inner)

    own_step, other_step = own_step_ref[...], other_step_ref[...]
    own_value, other_value = own_value_ref[...], other_value_ref[...]
    first_step = split(jnp.where(odd, other_step, own_step))
    second_step = split(jnp.where(odd, own_step, other_step))
    first = dot_rows(ahead, first_step, NT) + jnp.where(odd, other_value, own_value)
    second = dot_rows(first, second_step, NT) + jnp.where(odd, own_value, other_value)
    inner = dot_rows(back - second, second_step, NN)
    solved = dot_rows(
        jnp.where(odd, second - back, first - inner), split(inverse_ref[...]), NN
    )
    solution[...] = solved
    out_copies = [pltpu.make_async_copy(solution, solution_hbm, out_sems.at[comps])]
    out_copies[0].start()

    for comp in range(comps):
        for tile in range(section // 128):
            lanes = slice(tile * 128, (tile + 1) * 128)
            label = labels_ref[comp, :, lanes]
            weight = weight_ref[comp, :, lanes]
            for case in range(cases):
                table = jnp.broadcast_to(solved[case : case + 1, :], (layers, 128))
                spread = jnp.take_along_axis(table, label, axis=1, mode="promise_in_bounds")
                correction = weight * spread
                middle = slice(8, layers - 8)
                updated[case, comp, middle, lanes] = (
                    inner_base[case, comp, :, lanes] + correction[8 : layers - 8]
                )
                updated[case, comp, :8, lanes] = outer_base[case, comp, :8, lanes] + correction[:8]
                updated[case, comp, layers - 8 :, lanes] = (
                    outer_base[case, comp, 8:, lanes] + correction[layers - 8 :]
                )
        copy = pltpu.make_async_copy(
            updated.at[:, comp], updated_hbm.at[:, comp], out_sems.at[comp]
        )
        copy.start()
        out_copies.append(copy)
    for copy in out_copies:
        copy.wait()


def finish_call(strides, width, maps, shifts, levels, leaf, inner, outer, labels, weight):
    cases, comps, _, section = inner.shape
    layers = labels.shape[1]
    whole = (cases, comps, layers, section)
    order = maps[0].shape[1]
    ways = len(shifts)
    hbm, local = pl.BlockSpec(memory_space=pltpu.HBM), pl.BlockSpec(memory_space=pltpu.VMEM)
    before = (*maps, *shifts, *levels, *leaf)
    return pl.pallas_call(
        functools.partial(finish_kernel, strides, width, ways),
        in_specs=[local] * (len(before) + 4),
        out_specs=[hbm, hbm],
        out_shape=[
            jax.ShapeDtypeStruct(whole, f32),
            jax.ShapeDtypeStruct((cases, order), f32),
        ],
        scratch_shapes=[
            pltpu.VMEM((ways, 2 * order, order), f32),
            pltpu.VMEM((ways, 2 * cases, order), f32),
            pltpu.VMEM((ways, cases, order), f32),
            pltpu.VMEM((ways, cases, order), f32),
            pltpu.VMEM(whole, f32),
            pltpu.VMEM((cases, order), f32),
            pltpu.SemaphoreType.DMA((comps + 1,)),
        ],
        compiler_params=small(10),
        name="finish",
    )(*before, inner, outer, labels, weight)


def per_device(
    displacement, loads, section_stiffness, modulus, aggregate, basis_weight, diag_inverse, sub_factor
):
    count = lax.axis_size("row")
    ways = 4
    width = count // ways

    def swap(value, mask):
        return lax.ppermute(value, "row", [(i, i ^ mask) for i in range(count)])

    step, near, far = start_call(diag_inverse, sub_factor, displacement)
    other_step = swap(step, 1)
    near = swap(near, 1)
    far = lax.ppermute(
        far, "row", [(i, i + 1 if i & 1 else i - 1) for i in range(1, count - 1)]
    )
    cases, comps, layers, section = displacement.shape
    order = diag_inverse.shape[0]
    outer = (comps, cases, 16, section)
    node_values = (modulus, aggregate, basis_weight)
    inner_base, outer_across, diagonal, total = residual_call(
        inner_kernel,
        False,
        [
            (cases, comps, layers - 16, section),
            outer,
            (comps, 8, section),
            (4 * cases, order // 2),
        ],
        [pltpu.VMEM((comps, cases, layers - 16, section), f32)],
        displacement, loads, section_stiffness, *node_values,
    )
    maps, mixed = maps_call(pair_maps_kernel, "pair_maps", 1, step, other_step)
    pair_operands = (step, other_step, maps, mixed)
    strides, joins = [], []
    stride = 2
    while stride < width:
        other_maps = swap(maps, stride)
        if not strides:
            other_maps, total = lax.optimization_barrier((other_maps, total))
        joined, mixed, half = maps_call(
            functools.partial(join_maps_kernel, stride), "join_maps", 2, maps, other_maps
        )
        strides.append(stride)
        joins.append((maps, other_maps, mixed))
        maps = joined
        stride *= 2
    halves = [swap(half, hop * width) for hop in range(1, ways)]
    outer_base, value = residual_call(
        outer_kernel,
        True,
        [(cases, comps, 16, section), (cases, order)],
        [],
        displacement, loads, *node_values, diag_inverse, near, far, outer_across, diagonal, total,
    )
    other_value = swap(value, 1)
    shifts = shifts_call(pair_shifts_kernel, "pair_shifts", cases, value, other_value, *pair_operands)
    levels = []
    for stride, (own_maps, other_maps, mixed) in zip(strides, joins):
        other_shifts = swap(shifts, stride)
        levels += [own_maps, other_maps, shifts, other_shifts]
        shifts = shifts_call(
            functools.partial(join_shifts_kernel, stride), "join_shifts", cases,
            shifts, other_shifts, own_maps, other_maps, mixed,
        )
    shifts, *halves = lax.optimization_barrier((shifts, *halves))
    all_maps = [maps]
    for half in halves:
        all_maps += [half, swap(half, 1)]
    all_shifts = [shifts] + [swap(shifts, hop * width) for hop in range(1, ways)]
    leaf = (step, other_step, value, other_value, diag_inverse)
    updated, solution_rows = finish_call(
        tuple(strides), width, all_maps, all_shifts, levels, leaf, inner_base, outer_base, aggregate,
        basis_weight,
    )
    return updated, solution_rows.T


def solution(mesh):
    placed = (
        P("groups", None, "row", None),
        P("groups", None, "row", None),
        P("groups", None, None),
        P("row", "groups"),
        P("groups", "row", None),
        P("groups", "row", None),
        P("row", "groups"),
        P("row", "groups"),
    )
    return jax.shard_map(
        per_device,
        mesh=mesh,
        in_specs=placed,
        out_specs=(P("groups", None, "row", None), P("row", "groups")),
        check_vma=False,
    )
```

```python
import functools

import jax
import jax.numpy as jnp
from jax import lax
from jax.experimental import pallas as pl
from jax.experimental.pallas import tpu as pltpu
from jax.sharding import PartitionSpec as P

span_weights = (1.5, -0.15, 1.0 / 90.0)
hop_order = (0, 1, 3, 2)
bf16, f32 = jnp.bfloat16, jnp.float32
NN = (((1,), (0,)), ((), ()))
NT = (((1,), (1,)), ((), ()))
TN = (((0,), (0,)), ((), ()))


def split(value):
    high = value.astype(bf16)
    return high, (value - high.astype(f32)).astype(bf16)


def dot(left, right, dims):
    return lax.dot_general(left, right, dims, preferred_element_type=f32)


def dot3(left, right, dims):
    left_high, left_low = left
    right_high, right_low = right
    return dot(left_high, right_high, dims) + (
        dot(left_high, right_low, dims) + dot(left_low, right_high, dims)
    )


def dot_rows(rows, weights, dims):
    high, low = split(rows)
    weight_high, weight_low = weights
    count = rows.shape[0]
    both = dot(jnp.concatenate([high, low], axis=0), weight_high, dims)
    return both[:count] + both[count:] + dot(high, weight_low, dims)


def node_rows(edge, layers):
    return (0, layers - 8) if edge else tuple(range(8, layers - 8, 8))


def residual_part(
    edge, disp_ref, loads_ref, modulus_ref, labels_ref, weight_ref, across_ref, diagonal_of, padded,
    weighted, base_ref, comp, total,
):
    cases, comps, layers, section = disp_ref.shape
    tiles = section // 128
    groups = node_rows(edge, layers)
    depth = 8 * len(groups)
    stride = weighted.shape[1] // cases
    fine = total.shape[1]
    parts = total.shape[0] // (2 * cases)
    bins = lax.broadcasted_iota(jnp.int32, (fine, 128), 0).astype(f32).astype(bf16)
    for at, first in enumerate(groups):
        rows = slice(first, first + 8)
        out = slice(at * 8, at * 8 + 8)
        for tile in range(tiles):
            lanes = slice(tile * 128, (tile + 1) * 128)
            modulus = modulus_ref[rows, lanes]
            diagonal = diagonal_of(comp, lanes)
            inverse = 1.0 / (modulus * (2.0 * sum(span_weights)) + diagonal)
            weight = weight_ref[comp, rows, lanes]
            for case in range(cases):
                own = padded[comp, case, tile, 8 + first : 16 + first, :]
                span_sum = (2.0 * sum(span_weights)) * own
                for offset in range(1, 4):
                    low = padded[comp, case, tile, 8 + first - offset : 16 + first - offset, :]
                    high = padded[comp, case, tile, 8 + first + offset : 16 + first + offset, :]
                    span_sum = span_sum - span_weights[offset - 1] * (low + high)
                residual = loads_ref[case, comp, rows, lanes] - (
                    modulus * span_sum + across_ref[comp, case, out, lanes]
                )
                base_ref[case, comp, out, lanes] = own + residual * inverse
                start = case * stride + tile * depth + at * 8
                weighted[comp, start : start + 8, :] = weight * residual

    def restrict(group, total):
        at = pl.multiple_of(group * 8, 8)
        first = pl.multiple_of(groups[0] + group * (groups[1] - groups[0]), 8)
        block = labels_ref[comp, pl.ds(first, 8), :]
        big = lax.shift_right_logical(block, fine.bit_length() - 1).astype(f32)
        little = (block & (fine - 1)).astype(f32)
        for inner in range(8):
            onehots, values = [], []
            for tile in range(tiles):
                lanes = slice(tile * 128, (tile + 1) * 128)
                low = jnp.broadcast_to(little[inner : inner + 1, lanes], (16, 128)).astype(bf16)
                low = jnp.concatenate([low] * (fine // 16), axis=0)
                onehots.append(jnp.where(low == bins, bf16(1), bf16(0)))
                high = jnp.broadcast_to(big[inner : inner + 1, lanes], (16, 128)).astype(bf16)
                value = weighted[comp, pl.ds(tile * depth + at + inner, cases, stride=stride), :]
                value = jnp.concatenate(split(value), axis=0)
                values.append(
                    jnp.concatenate(
                        [jnp.where(high == bf16(part), value, bf16(0)) for part in range(parts)],
                        axis=0,
                    )
                )
            total = total + dot(
                jnp.concatenate(values, axis=1), jnp.concatenate(onehots, axis=1), NT
            )
        return total

    return lax.fori_loop(0, len(groups), restrict, total)


def inner_kernel(
    disp_ref, loads_ref, section_ref, modulus_ref, labels_ref, weight_ref,
    base_ref, outer_ref, diagonal_ref, total_ref, padded, weighted, across_ref,
):
    cases, comps, layers, section = disp_ref.shape
    tiles = section // 128
    same = lax.broadcasted_iota(jnp.int32, (128, 128), 0) == lax.broadcasted_iota(
        jnp.int32, (128, 128), 1
    )
    total = jnp.zeros(total_ref.shape, f32)
    for comp in range(comps):
        for tile in range(tiles):
            lanes = slice(tile * 128, (tile + 1) * 128)
            padded[comp, :, tile, 8 : 8 + layers, :] = disp_ref[:, comp, :, lanes]
        high, low = split(disp_ref[:, comp].reshape(cases * layers, section))
        section_high, section_low = split(section_ref[comp])
        across = dot(
            jnp.concatenate([high, high, low], axis=1),
            jnp.concatenate([section_high, section_low, section_high], axis=0),
            NN,
        ).reshape(cases, layers, section)
        across_ref[comp] = across[:, 8 : layers - 8]
        outer_ref[comp, :, :8] = across[:, :8]
        outer_ref[comp, :, 8:] = across[:, layers - 8 :]
        diagonals = []
        for tile in range(tiles):
            lanes = slice(tile * 128, (tile + 1) * 128)
            block = section_ref[comp, lanes, lanes]
            diagonals.append(jnp.sum(jnp.where(same, block, 0.0), axis=0, keepdims=True))
            diagonal_ref[comp, :, lanes] = jnp.broadcast_to(diagonals[-1], (8, 128))
        total = residual_part(
            False, disp_ref, loads_ref, modulus_ref, labels_ref, weight_ref, across_ref,
            lambda _, lanes: diagonals[lanes.start // 128], padded, weighted, base_ref, comp, total,
        )
    total_ref[...] = total


def outer_kernel(
    disp_ref, loads_ref, modulus_ref, labels_ref, weight_ref, inverse_ref, near_ref, far_ref,
    across_ref, diagonal_ref, inner_total_ref, base_ref, value_ref, padded, weighted,
):
    cases, comps, layers, section = disp_ref.shape
    mine = lax.axis_index("row")
    odd = (mine & 1) == 1
    lowest, highest = mine == 0, mine == lax.axis_size("row") - 1
    tiles = section // 128
    total = inner_total_ref[...]
    for comp in range(comps):
        for tile in range(tiles):
            lanes = slice(tile * 128, (tile + 1) * 128)
            padded[comp, :, tile, 8:24, :] = disp_ref[:, comp, :16, lanes]
            padded[comp, :, tile, layers - 8 : layers + 8, :] = disp_ref[
                :, comp, layers - 16 :, lanes
            ]
            for row in range(3):
                at = (tile * 3 + row) * cases * comps + comp * cases
                near, far = near_ref[at : at + cases, :], far_ref[at : at + cases, :]
                below = jnp.where(lowest, 0.0, jnp.where(odd, near, far))
                above = jnp.where(highest, 0.0, jnp.where(odd, far, near))
                for case in range(cases):
                    padded[comp, case, tile, 5 + row : 6 + row, :] = below[case : case + 1]
                    low = 8 + layers + row
                    padded[comp, case, tile, low : low + 1, :] = above[case : case + 1]
        total = residual_part(
            True, disp_ref, loads_ref, modulus_ref, labels_ref, weight_ref, across_ref,
            lambda comp, lanes: diagonal_ref[comp, :, lanes], padded, weighted, base_ref, comp,
            total,
        )
    sums = []
    for at in range(0, total.shape[0], 2 * cases):
        sums.append(total[at : at + cases] + total[at + cases : at + 2 * cases])
    value_ref[...] = dot_rows(jnp.concatenate(sums, axis=1), split(inverse_ref[...]), NT)


def residual_call(kernel, edge, out_shape, scratch_shapes, *operands):
    cases, comps, layers, section = operands[0].shape
    tiles = section // 128
    depth = 8 * len(node_rows(edge, layers))
    local = pl.BlockSpec(memory_space=pltpu.VMEM)
    return pl.pallas_call(
        kernel,
        in_specs=[local] * len(operands),
        out_specs=[local] * len(out_shape),
        out_shape=[jax.ShapeDtypeStruct(shape, f32) for shape in out_shape],
        scratch_shapes=[
            pltpu.VMEM((comps, cases, tiles, layers + 16, 128), f32),
            pltpu.VMEM((comps, cases * (tiles * depth + 8), 128), f32),
            *scratch_shapes,
        ],
        compiler_params=pltpu.CompilerParams(vmem_limit_bytes=14 << 20),
        cost_estimate=pl.CostEstimate(
            flops=3 * cases * comps * layers * section * section,
            bytes_accessed=8 * operands[0].size,
            transcendentals=0,
        ),
        name="outer_residual" if edge else "inner_residual",
    )(*operands)


def small(limit):
    return pltpu.CompilerParams(vmem_limit_bytes=limit << 20)


def in_hbm(*values):
    return [pltpu.with_memory_space_constraint(value, pltpu.HBM) for value in values]


def start_kernel(
    inverse_hbm, sub_hbm, disp_hbm, step_ref, near_ref, far_ref, inverse, sub, first, last, sems
):
    cases, comps, rows, section = first.shape
    layers = disp_hbm.shape[2]
    copies = [
        pltpu.make_async_copy(inverse_hbm, inverse, sems.at[0]),
        pltpu.make_async_copy(sub_hbm, sub, sems.at[1]),
        pltpu.make_async_copy(disp_hbm.at[:, :, pl.ds(0, rows), :], first, sems.at[2]),
        pltpu.make_async_copy(disp_hbm.at[:, :, pl.ds(layers - rows, rows), :], last, sems.at[3]),
    ]
    for copy in copies:
        copy.start()
    odd = (lax.axis_index("row") & 1) == 1
    copies[0].wait()
    copies[1].wait()
    step_ref[...] = -dot3(split(inverse[...]), split(sub[...]), NN)
    copies[2].wait()
    copies[3].wait()
    for tile in range(section // 128):
        lanes = slice(tile * 128, (tile + 1) * 128)
        for row in range(3):
            for comp in range(comps):
                at = (tile * 3 + row) * cases * comps + comp * cases
                low = first[:, comp, row, lanes]
                high = last[:, comp, rows - 3 + row, lanes]
                near_ref[at : at + cases, :] = jnp.where(odd, low, high)
                far_ref[at : at + cases, :] = jnp.where(odd, high, low)


def start_call(diag_inverse, sub_factor, displacement):
    cases, comps, layers, section = displacement.shape
    packed = jax.ShapeDtypeStruct((cases * comps * 3 * section // 128, 128), f32)
    block = pltpu.VMEM((cases, comps, 8, section), f32)
    square = pltpu.VMEM(diag_inverse.shape, f32)
    return pl.pallas_call(
        start_kernel,
        in_specs=[pl.BlockSpec(memory_space=pltpu.HBM)] * 3,
        out_specs=[pl.BlockSpec(memory_space=pltpu.VMEM)] * 3,
        out_shape=[jax.ShapeDtypeStruct(diag_inverse.shape, f32), packed, packed],
        scratch_shapes=[square, square, block, block, pltpu.SemaphoreType.DMA((4,))],
        compiler_params=small(4),
        cost_estimate=pl.CostEstimate(flops=10**10, bytes_accessed=10**6, transcendentals=0),
        name="start",
    )(*in_hbm(diag_inverse, sub_factor, displacement))


def pair_maps_kernel(own_ref, other_ref, maps_ref, mixed_ref):
    order = own_ref.shape[0]
    odd = (lax.axis_index("row") & 1) == 1
    own, other = own_ref[...], other_ref[...]
    first = jnp.where(odd, other, own)
    first_split, second_split = split(first), split(jnp.where(odd, own, other))
    phi = dot3(second_split, first_split, NN)
    phi_split = split(phi)
    gram = dot3(first_split, first_split, TN) + dot3(phi_split, phi_split, TN)
    maps_ref[:order, :] = phi
    maps_ref[order:, :] = gram
    mixed_ref[...] = first + dot3(second_split, phi_split, TN)


def join_maps_kernel(stride, own_ref, other_ref, maps_ref, mixed_ref, half_ref):
    order = own_ref.shape[1]
    upper = (lax.axis_index("row") & stride) != 0
    own, other = own_ref[...], other_ref[...]
    first, second = jnp.where(upper, other, own), jnp.where(upper, own, other)
    first_phi = split(first[:order])
    mixed = dot3(split(second[order:]), first_phi, NN)
    phi = dot3(split(second[:order]), first_phi, NN)
    gram = first[order:] + dot3(first_phi, split(mixed), TN)
    maps_ref[:order, :] = phi
    maps_ref[order:, :] = gram
    mixed_ref[...] = mixed
    odd = (lax.axis_index("row") & 1) == 1
    half_ref[...] = jnp.where(odd, gram, phi)


def maps_call(kernel, name, extra, own, other):
    order = own.shape[1]
    return pl.pallas_call(
        kernel,
        out_shape=[
            jax.ShapeDtypeStruct((2 * order, order), f32),
        ]
        + [jax.ShapeDtypeStruct((order, order), f32)] * extra,
        compiler_params=small(3),
        cost_estimate=pl.CostEstimate(flops=10**10, bytes_accessed=10**6, transcendentals=0),
        name=name,
    )(own, other)


def pair_shifts_kernel(own_ref, other_ref, own_step_ref, other_step_ref, maps_ref, mixed_ref, out_ref):
    cases, order = own_ref.shape
    odd = (lax.axis_index("row") & 1) == 1
    own, other = own_ref[...], other_ref[...]
    first, second = jnp.where(odd, other, own), jnp.where(odd, own, other)
    second_step = jnp.where(odd, own_step_ref[...], other_step_ref[...])
    out_ref[:cases, :] = dot_rows(first, split(second_step), NT) + second
    out_ref[cases:, :] = -(
        dot_rows(first, split(mixed_ref[...]), NN)
        + dot_rows(second, split(maps_ref[:order, :]), NN)
    )


def join_shifts_kernel(stride, own_ref, other_ref, own_maps_ref, other_maps_ref, mixed_ref, out_ref):
    order = mixed_ref.shape[0]
    cases = own_ref.shape[0] // 2
    upper = (lax.axis_index("row") & stride) != 0
    own, other = own_ref[...], other_ref[...]
    first, second = jnp.where(upper, other, own), jnp.where(upper, own, other)
    own_phi, other_phi = own_maps_ref[:order, :], other_maps_ref[:order, :]
    first_phi = jnp.where(upper, other_phi, own_phi)
    second_phi = jnp.where(upper, own_phi, other_phi)
    out_ref[:cases, :] = dot_rows(first[:cases], split(second_phi), NT) + second[:cases]
    out_ref[cases:, :] = (
        first[cases:]
        + dot_rows(second[cases:], split(first_phi), NN)
        - dot_rows(first[:cases], split(mixed_ref[...]), NN)
    )


def shifts_call(kernel, name, cases, *operands):
    return pl.pallas_call(
        kernel,
        out_shape=jax.ShapeDtypeStruct((2 * cases, operands[0].shape[1]), f32),
        compiler_params=small(3),
        name=name,
    )(*operands)


def finish_kernel(strides, width, ways, *refs):
    own_maps_ref, got_ref, swapped_ref, *refs = refs
    order = own_maps_ref.shape[1]
    shifts, refs = refs[:ways], refs[ways:]
    levels = []
    for stride in strides:
        levels.append((stride, *refs[:4]))
        refs = refs[4:]
    (own_step_ref, other_step_ref, own_value_ref, other_value_ref, inverse_ref, inner_base, outer_base,
     labels_ref,
     weight_ref, updated_hbm, solution_hbm, all_maps, all_shifts, ahead_ref, back_ref, updated,
     solution, out_sems) = refs
    cases = own_value_ref.shape[0]
    comps, layers, section = labels_ref.shape
    mine = lax.axis_index("row")
    odd = (mine & 1) == 1
    group = mine // width

    all_maps[group] = own_maps_ref[...]
    for hop in range(1, ways):
        part = slice((hop - 1) * order, hop * order)
        got, swapped = got_ref[part, :], swapped_ref[part, :]
        all_maps[group ^ hop, :order] = jnp.where(odd, swapped, got)
        all_maps[group ^ hop, order:] = jnp.where(odd, got, swapped)
    for hop in range(ways):
        all_shifts[group ^ hop_order[hop]] = shifts[hop][...]

    ahead = all_shifts[0, :cases]
    ahead_ref[0] = jnp.zeros_like(ahead)
    ahead_ref[1] = ahead
    for at in range(1, ways - 1):
        ahead = dot_rows(ahead, split(all_maps[at, :order]), NT) + all_shifts[at, :cases]
        ahead_ref[at + 1] = ahead
    back = jnp.zeros_like(ahead)
    back_ref[ways - 1] = back
    for at in range(ways - 1, 0, -1):
        own = all_shifts[at, cases:] - dot_rows(ahead_ref[at], split(all_maps[at, order:]), NN)
        last = at == ways - 1
        back = own if last else own + dot_rows(back, split(all_maps[at, :order]), NN)
        back_ref[at - 1] = back
    ahead, back = ahead_ref[group], back_ref[group]

    for stride, own_maps, other_maps, own_shifts, other_shifts in levels[::-1]:
        upper = (mine & stride) != 0
        first_phi = jnp.where(upper, other_maps[:order, :], own_maps[:order, :])
        second_maps = jnp.where(upper, own_maps[...], other_maps[...])
        own, other = own_shifts[...], other_shifts[...]
        first_shift = jnp.where(upper, other[:cases], own[:cases])
        second_shift = jnp.where(upper, own[cases:], other[cases:])
        middle = dot_rows(ahead, split(first_phi), NT) + first_shift
        inner = (
            dot_rows(back, split(second_maps[:order]), NN)
            - dot_rows(middle, split(second_maps[order:]), NN)
            + second_shift
        )
        ahead = jnp.where(upper, middle, ahead)
        back = jnp.where(upper, back, inner)

    own_step, other_step = own_step_ref[...], other_step_ref[...]
    own_value, other_value = own_value_ref[...], other_value_ref[...]
    first_step = split(jnp.where(odd, other_step, own_step))
    second_step = split(jnp.where(odd, own_step, other_step))
    first = dot_rows(ahead, first_step, NT) + jnp.where(odd, other_value, own_value)
    second = dot_rows(first, second_step, NT) + jnp.where(odd, own_value, other_value)
    inner = dot_rows(back - second, second_step, NN)
    solved = dot_rows(
        jnp.where(odd, second - back, first - inner), split(inverse_ref[...]), NN
    )
    solution[...] = solved
    out_copies = [pltpu.make_async_copy(solution, solution_hbm, out_sems.at[comps])]
    out_copies[0].start()

    for comp in range(comps):
        for tile in range(section // 128):
            lanes = slice(tile * 128, (tile + 1) * 128)
            label = labels_ref[comp, :, lanes]
            weight = weight_ref[comp, :, lanes]
            for case in range(cases):
                table = jnp.broadcast_to(solved[case : case + 1, :], (layers, 128))
                spread = jnp.take_along_axis(table, label, axis=1, mode="promise_in_bounds")
                correction = weight * spread
                middle = slice(8, layers - 8)
                updated[case, comp, middle, lanes] = (
                    inner_base[case, comp, :, lanes] + correction[8 : layers - 8]
                )
                updated[case, comp, :8, lanes] = outer_base[case, comp, :8, lanes] + correction[:8]
                updated[case, comp, layers - 8 :, lanes] = (
                    outer_base[case, comp, 8:, lanes] + correction[layers - 8 :]
                )
        copy = pltpu.make_async_copy(
            updated.at[:, comp], updated_hbm.at[:, comp], out_sems.at[comp]
        )
        copy.start()
        out_copies.append(copy)
    for copy in out_copies:
        copy.wait()


def finish_call(strides, width, maps, shifts, levels, leaf, inner, outer, labels, weight):
    cases, comps, _, section = inner.shape
    layers = labels.shape[1]
    whole = (cases, comps, layers, section)
    order = maps[0].shape[1]
    ways = len(shifts)
    hbm, local = pl.BlockSpec(memory_space=pltpu.HBM), pl.BlockSpec(memory_space=pltpu.VMEM)
    before = (*maps, *[shifts[hop] for hop in hop_order], *levels, *leaf)
    return pl.pallas_call(
        functools.partial(finish_kernel, strides, width, ways),
        in_specs=[local] * (len(before) + 4),
        out_specs=[hbm, hbm],
        out_shape=[
            jax.ShapeDtypeStruct(whole, f32),
            jax.ShapeDtypeStruct((cases, order), f32),
        ],
        scratch_shapes=[
            pltpu.VMEM((ways, 2 * order, order), f32),
            pltpu.VMEM((ways, 2 * cases, order), f32),
            pltpu.VMEM((ways, cases, order), f32),
            pltpu.VMEM((ways, cases, order), f32),
            pltpu.VMEM(whole, f32),
            pltpu.VMEM((cases, order), f32),
            pltpu.SemaphoreType.DMA((comps + 1,)),
        ],
        compiler_params=small(10),
        name="finish",
    )(*before, inner, outer, labels, weight)


def per_device(
    displacement, loads, section_stiffness, modulus, aggregate, basis_weight, diag_inverse, sub_factor
):
    count = lax.axis_size("row")
    ways = 4
    width = count // ways

    def swap(value, mask):
        return lax.ppermute(value, "row", [(i, i ^ mask) for i in range(count)])

    step, near, far = start_call(diag_inverse, sub_factor, displacement)
    other_step = swap(step, 1)
    near = swap(near, 1)
    far = lax.ppermute(
        far, "row", [(i, i + 1 if i & 1 else i - 1) for i in range(1, count - 1)]
    )
    cases, comps, layers, section = displacement.shape
    order = diag_inverse.shape[0]
    outer = (comps, cases, 16, section)
    node_values = (modulus, aggregate, basis_weight)
    inner_base, outer_across, diagonal, total = residual_call(
        inner_kernel,
        False,
        [
            (cases, comps, layers - 16, section),
            outer,
            (comps, 8, section),
            (4 * cases, order // 2),
        ],
        [pltpu.VMEM((comps, cases, layers - 16, section), f32)],
        displacement, loads, section_stiffness, *node_values,
    )
    maps, mixed = maps_call(pair_maps_kernel, "pair_maps", 1, step, other_step)
    pair_operands = (step, other_step, maps, mixed)
    strides, joins = [], []
    stride = 2
    while stride < width:
        other_maps = swap(maps, stride)
        if not strides:
            other_maps, total = lax.optimization_barrier((other_maps, total))
        joined, mixed, half = maps_call(
            functools.partial(join_maps_kernel, stride), "join_maps", 2, maps, other_maps
        )
        strides.append(stride)
        joins.append((maps, other_maps, mixed))
        maps = joined
        stride *= 2
    halves = [swap(half, hop * width) for hop in range(1, ways)]
    outer_base, value = residual_call(
        outer_kernel,
        True,
        [(cases, comps, 16, section), (cases, order)],
        [],
        displacement, loads, *node_values, diag_inverse, near, far, outer_across, diagonal, total,
    )
    other_value = swap(value, 1)
    shifts = shifts_call(pair_shifts_kernel, "pair_shifts", cases, value, other_value, *pair_operands)
    levels = []
    for stride, (own_maps, other_maps, mixed) in zip(strides, joins):
        other_shifts = swap(shifts, stride)
        levels += [own_maps, other_maps, shifts, other_shifts]
        shifts = shifts_call(
            functools.partial(join_shifts_kernel, stride), "join_shifts", cases,
            shifts, other_shifts, own_maps, other_maps, mixed,
        )
    gathered = jnp.concatenate(lax.optimization_barrier((shifts, *halves))[1:], axis=0)
    all_maps = [maps, gathered, swap(gathered, 1)]
    all_shifts = [shifts] + [swap(shifts, hop * width) for hop in range(1, ways)]
    leaf = (step, other_step, value, other_value, diag_inverse)
    updated, solution_rows = finish_call(
        tuple(strides), width, all_maps, all_shifts, levels, leaf, inner_base, outer_base, aggregate,
        basis_weight,
    )
    return updated, solution_rows.T


def solution(mesh):
    placed = (
        P("groups", None, "row", None),
        P("groups", None, "row", None),
        P("groups", None, None),
        P("row", "groups"),
        P("groups", "row", None),
        P("groups", "row", None),
        P("row", "groups"),
        P("row", "groups"),
    )
    return jax.shard_map(
        per_device,
        mesh=mesh,
        in_specs=placed,
        out_specs=(P("groups", None, "row", None), P("row", "groups")),
        check_vma=False,
    )
```

```python
import functools

import jax
import jax.numpy as jnp
from jax import lax
from jax.experimental import pallas as pl
from jax.experimental.pallas import tpu as pltpu
from jax.sharding import PartitionSpec as P

span_weights = (1.5, -0.15, 1.0 / 90.0)
hop_order = (0, 1, 3, 2)
bf16, f32 = jnp.bfloat16, jnp.float32
NN = (((1,), (0,)), ((), ()))
NT = (((1,), (1,)), ((), ()))
TN = (((0,), (0,)), ((), ()))


def split(value):
    high = value.astype(bf16)
    return high, (value - high.astype(f32)).astype(bf16)


def dot(left, right, dims):
    return lax.dot_general(left, right, dims, preferred_element_type=f32)


def dot3(left, right, dims):
    left_high, left_low = left
    right_high, right_low = right
    return dot(left_high, right_high, dims) + (
        dot(left_high, right_low, dims) + dot(left_low, right_high, dims)
    )


def dot_rows(rows, weights, dims):
    high, low = split(rows)
    count = rows.shape[0]
    left = jnp.concatenate(
        [
            jnp.concatenate([high, high], axis=1),
            jnp.concatenate([low, jnp.zeros_like(low)], axis=1),
        ],
        axis=0,
    )
    both = dot(left, jnp.concatenate(weights, axis=dims[0][1][0]), dims)
    return both[:count] + both[count:]


def node_rows(edge, layers):
    return (0, layers - 8) if edge else tuple(range(8, layers - 8, 8))


def residual_part(
    edge, disp_ref, loads_ref, modulus_ref, labels_ref, weight_ref, across_ref, diagonal_of, padded,
    weighted, base_ref, comp, total,
):
    cases, comps, layers, section = disp_ref.shape
    tiles = section // 128
    groups = node_rows(edge, layers)
    depth = 8 * len(groups)
    stride = weighted.shape[1] // cases
    fine = total.shape[1]
    parts = total.shape[0] // (2 * cases)
    bins = lax.broadcasted_iota(jnp.int32, (fine, 128), 0).astype(f32).astype(bf16)
    for at, first in enumerate(groups):
        rows = slice(first, first + 8)
        out = slice(at * 8, at * 8 + 8)
        for tile in range(tiles):
            lanes = slice(tile * 128, (tile + 1) * 128)
            modulus = modulus_ref[rows, lanes]
            diagonal = diagonal_of(comp, lanes)
            inverse = 1.0 / (modulus * (2.0 * sum(span_weights)) + diagonal)
            weight = weight_ref[comp, rows, lanes]
            for case in range(cases):
                own = padded[comp, case, tile, 8 + first : 16 + first, :]
                span_sum = (2.0 * sum(span_weights)) * own
                for offset in range(1, 4):
                    low = padded[comp, case, tile, 8 + first - offset : 16 + first - offset, :]
                    high = padded[comp, case, tile, 8 + first + offset : 16 + first + offset, :]
                    span_sum = span_sum - span_weights[offset - 1] * (low + high)
                residual = loads_ref[case, comp, rows, lanes] - (
                    modulus * span_sum + across_ref[comp, case, out, lanes]
                )
                base_ref[case, comp, out, lanes] = own + residual * inverse
                start = case * stride + tile * depth + at * 8
                weighted[comp, start : start + 8, :] = weight * residual

    def restrict(group, total):
        at = pl.multiple_of(group * 8, 8)
        first = pl.multiple_of(groups[0] + group * (groups[1] - groups[0]), 8)
        block = labels_ref[comp, pl.ds(first, 8), :]
        big = lax.shift_right_logical(block, fine.bit_length() - 1).astype(f32)
        little = (block & (fine - 1)).astype(f32)
        for inner in range(8):
            onehots, values = [], []
            for tile in range(tiles):
                lanes = slice(tile * 128, (tile + 1) * 128)
                low = jnp.broadcast_to(little[inner : inner + 1, lanes], (16, 128)).astype(bf16)
                low = jnp.concatenate([low] * (fine // 16), axis=0)
                onehots.append(jnp.where(low == bins, bf16(1), bf16(0)))
                high = jnp.broadcast_to(big[inner : inner + 1, lanes], (16, 128)).astype(bf16)
                value = weighted[comp, pl.ds(tile * depth + at + inner, cases, stride=stride), :]
                value = jnp.concatenate(split(value), axis=0)
                values.append(
                    jnp.concatenate(
                        [jnp.where(high == bf16(part), value, bf16(0)) for part in range(parts)],
                        axis=0,
                    )
                )
            total = total + dot(
                jnp.concatenate(values, axis=1), jnp.concatenate(onehots, axis=1), NT
            )
        return total

    return lax.fori_loop(0, len(groups), restrict, total)


def inner_kernel(
    disp_ref, loads_ref, section_ref, modulus_ref, labels_ref, weight_ref,
    base_ref, outer_ref, diagonal_ref, total_ref, padded, weighted, across_ref,
):
    cases, comps, layers, section = disp_ref.shape
    tiles = section // 128
    same = lax.broadcasted_iota(jnp.int32, (128, 128), 0) == lax.broadcasted_iota(
        jnp.int32, (128, 128), 1
    )
    total = jnp.zeros(total_ref.shape, f32)
    for comp in range(comps):
        for tile in range(tiles):
            lanes = slice(tile * 128, (tile + 1) * 128)
            padded[comp, :, tile, 8 : 8 + layers, :] = disp_ref[:, comp, :, lanes]
        high, low = split(disp_ref[:, comp].reshape(cases * layers, section))
        section_high, section_low = split(section_ref[comp])
        across = dot(
            jnp.concatenate([high, high, low], axis=1),
            jnp.concatenate([section_high, section_low, section_high], axis=0),
            NN,
        ).reshape(cases, layers, section)
        across_ref[comp] = across[:, 8 : layers - 8]
        outer_ref[comp, :, :8] = across[:, :8]
        outer_ref[comp, :, 8:] = across[:, layers - 8 :]
        diagonals = []
        for tile in range(tiles):
            lanes = slice(tile * 128, (tile + 1) * 128)
            block = section_ref[comp, lanes, lanes]
            diagonals.append(jnp.sum(jnp.where(same, block, 0.0), axis=0, keepdims=True))
            diagonal_ref[comp, :, lanes] = jnp.broadcast_to(diagonals[-1], (8, 128))
        total = residual_part(
            False, disp_ref, loads_ref, modulus_ref, labels_ref, weight_ref, across_ref,
            lambda _, lanes: diagonals[lanes.start // 128], padded, weighted, base_ref, comp, total,
        )
    total_ref[...] = total


def outer_kernel(
    disp_ref, loads_ref, modulus_ref, labels_ref, weight_ref, inverse_ref, near_ref, far_ref,
    across_ref, diagonal_ref, inner_total_ref, base_ref, value_ref, padded, weighted,
):
    cases, comps, layers, section = disp_ref.shape
    mine = lax.axis_index("row")
    odd = (mine & 1) == 1
    lowest, highest = mine == 0, mine == lax.axis_size("row") - 1
    tiles = section // 128
    total = inner_total_ref[...]
    for comp in range(comps):
        for tile in range(tiles):
            lanes = slice(tile * 128, (tile + 1) * 128)
            padded[comp, :, tile, 8:24, :] = disp_ref[:, comp, :16, lanes]
            padded[comp, :, tile, layers - 8 : layers + 8, :] = disp_ref[
                :, comp, layers - 16 :, lanes
            ]
            for row in range(3):
                at = (tile * 3 + row) * cases * comps + comp * cases
                near, far = near_ref[at : at + cases, :], far_ref[at : at + cases, :]
                below = jnp.where(lowest, 0.0, jnp.where(odd, near, far))
                above = jnp.where(highest, 0.0, jnp.where(odd, far, near))
                for case in range(cases):
                    padded[comp, case, tile, 5 + row : 6 + row, :] = below[case : case + 1]
                    low = 8 + layers + row
                    padded[comp, case, tile, low : low + 1, :] = above[case : case + 1]
        total = residual_part(
            True, disp_ref, loads_ref, modulus_ref, labels_ref, weight_ref, across_ref,
            lambda comp, lanes: diagonal_ref[comp, :, lanes], padded, weighted, base_ref, comp,
            total,
        )
    sums = []
    for at in range(0, total.shape[0], 2 * cases):
        sums.append(total[at : at + cases] + total[at + cases : at + 2 * cases])
    value_ref[...] = dot_rows(jnp.concatenate(sums, axis=1), split(inverse_ref[...]), NT)


def residual_call(kernel, edge, out_shape, scratch_shapes, *operands):
    cases, comps, layers, section = operands[0].shape
    tiles = section // 128
    depth = 8 * len(node_rows(edge, layers))
    local = pl.BlockSpec(memory_space=pltpu.VMEM)
    return pl.pallas_call(
        kernel,
        in_specs=[local] * len(operands),
        out_specs=[local] * len(out_shape),
        out_shape=[jax.ShapeDtypeStruct(shape, f32) for shape in out_shape],
        scratch_shapes=[
            pltpu.VMEM((comps, cases, tiles, layers + 16, 128), f32),
            pltpu.VMEM((comps, cases * (tiles * depth + 8), 128), f32),
            *scratch_shapes,
        ],
        compiler_params=pltpu.CompilerParams(vmem_limit_bytes=14 << 20),
        cost_estimate=pl.CostEstimate(
            flops=3 * cases * comps * layers * section * section,
            bytes_accessed=8 * operands[0].size,
            transcendentals=0,
        ),
        name="outer_residual" if edge else "inner_residual",
    )(*operands)


def small(limit):
    return pltpu.CompilerParams(vmem_limit_bytes=limit << 20)


def in_hbm(*values):
    return [pltpu.with_memory_space_constraint(value, pltpu.HBM) for value in values]


def start_kernel(
    inverse_hbm, sub_hbm, disp_hbm, step_ref, near_ref, far_ref, inverse, sub, first, last, sems
):
    cases, comps, rows, section = first.shape
    layers = disp_hbm.shape[2]
    copies = [
        pltpu.make_async_copy(inverse_hbm, inverse, sems.at[0]),
        pltpu.make_async_copy(sub_hbm, sub, sems.at[1]),
        pltpu.make_async_copy(disp_hbm.at[:, :, pl.ds(0, rows), :], first, sems.at[2]),
        pltpu.make_async_copy(disp_hbm.at[:, :, pl.ds(layers - rows, rows), :], last, sems.at[3]),
    ]
    for copy in copies:
        copy.start()
    odd = (lax.axis_index("row") & 1) == 1
    copies[0].wait()
    copies[1].wait()
    step_ref[...] = -dot3(split(inverse[...]), split(sub[...]), NN)
    copies[2].wait()
    copies[3].wait()
    for tile in range(section // 128):
        lanes = slice(tile * 128, (tile + 1) * 128)
        for row in range(3):
            for comp in range(comps):
                at = (tile * 3 + row) * cases * comps + comp * cases
                low = first[:, comp, row, lanes]
                high = last[:, comp, rows - 3 + row, lanes]
                near_ref[at : at + cases, :] = jnp.where(odd, low, high)
                far_ref[at : at + cases, :] = jnp.where(odd, high, low)


def start_call(diag_inverse, sub_factor, displacement):
    cases, comps, layers, section = displacement.shape
    packed = jax.ShapeDtypeStruct((cases * comps * 3 * section // 128, 128), f32)
    block = pltpu.VMEM((cases, comps, 8, section), f32)
    square = pltpu.VMEM(diag_inverse.shape, f32)
    return pl.pallas_call(
        start_kernel,
        in_specs=[pl.BlockSpec(memory_space=pltpu.HBM)] * 3,
        out_specs=[pl.BlockSpec(memory_space=pltpu.VMEM)] * 3,
        out_shape=[jax.ShapeDtypeStruct(diag_inverse.shape, f32), packed, packed],
        scratch_shapes=[square, square, block, block, pltpu.SemaphoreType.DMA((4,))],
        compiler_params=small(4),
        cost_estimate=pl.CostEstimate(flops=10**10, bytes_accessed=10**6, transcendentals=0),
        name="start",
    )(*in_hbm(diag_inverse, sub_factor, displacement))


def pair_maps_kernel(own_ref, other_ref, maps_ref, mixed_ref):
    order = own_ref.shape[0]
    odd = (lax.axis_index("row") & 1) == 1
    own, other = own_ref[...], other_ref[...]
    first = jnp.where(odd, other, own)
    first_split, second_split = split(first), split(jnp.where(odd, own, other))
    phi = dot3(second_split, first_split, NN)
    phi_split = split(phi)
    gram = dot3(first_split, first_split, TN) + dot3(phi_split, phi_split, TN)
    maps_ref[:order, :] = phi
    maps_ref[order:, :] = gram
    mixed_ref[...] = first + dot3(second_split, phi_split, TN)


def join_maps_kernel(stride, own_ref, other_ref, maps_ref, mixed_ref, half_ref):
    order = own_ref.shape[1]
    upper = (lax.axis_index("row") & stride) != 0
    own, other = own_ref[...], other_ref[...]
    first, second = jnp.where(upper, other, own), jnp.where(upper, own, other)
    first_phi = split(first[:order])
    mixed = dot3(split(second[order:]), first_phi, NN)
    phi = dot3(split(second[:order]), first_phi, NN)
    gram = first[order:] + dot3(first_phi, split(mixed), TN)
    maps_ref[:order, :] = phi
    maps_ref[order:, :] = gram
    mixed_ref[...] = mixed
    odd = (lax.axis_index("row") & 1) == 1
    half_ref[...] = jnp.where(odd, gram, phi)


def maps_call(kernel, name, extra, own, other):
    order = own.shape[1]
    return pl.pallas_call(
        kernel,
        out_shape=[
            jax.ShapeDtypeStruct((2 * order, order), f32),
        ]
        + [jax.ShapeDtypeStruct((order, order), f32)] * extra,
        compiler_params=small(3),
        cost_estimate=pl.CostEstimate(flops=10**10, bytes_accessed=10**6, transcendentals=0),
        name=name,
    )(own, other)


def pair_shifts_kernel(own_ref, other_ref, own_step_ref, other_step_ref, maps_ref, mixed_ref, out_ref):
    cases, order = own_ref.shape
    odd = (lax.axis_index("row") & 1) == 1
    own, other = own_ref[...], other_ref[...]
    first, second = jnp.where(odd, other, own), jnp.where(odd, own, other)
    second_step = jnp.where(odd, own_step_ref[...], other_step_ref[...])
    out_ref[:cases, :] = dot_rows(first, split(second_step), NT) + second
    out_ref[cases:, :] = -(
        dot_rows(first, split(mixed_ref[...]), NN)
        + dot_rows(second, split(maps_ref[:order, :]), NN)
    )


def join_shifts_kernel(stride, own_ref, other_ref, own_maps_ref, other_maps_ref, mixed_ref, out_ref):
    order = mixed_ref.shape[0]
    cases = own_ref.shape[0] // 2
    upper = (lax.axis_index("row") & stride) != 0
    own, other = own_ref[...], other_ref[...]
    first, second = jnp.where(upper, other, own), jnp.where(upper, own, other)
    own_phi, other_phi = own_maps_ref[:order, :], other_maps_ref[:order, :]
    first_phi = jnp.where(upper, other_phi, own_phi)
    second_phi = jnp.where(upper, own_phi, other_phi)
    out_ref[:cases, :] = dot_rows(first[:cases], split(second_phi), NT) + second[:cases]
    out_ref[cases:, :] = (
        first[cases:]
        + dot_rows(second[cases:], split(first_phi), NN)
        - dot_rows(first[:cases], split(mixed_ref[...]), NN)
    )


def shifts_call(kernel, name, cases, *operands):
    return pl.pallas_call(
        kernel,
        out_shape=jax.ShapeDtypeStruct((2 * cases, operands[0].shape[1]), f32),
        compiler_params=small(3),
        name=name,
    )(*operands)


def local_kernel(strides, *refs):
    levels = []
    for stride in strides:
        levels.append((stride, *refs[:4]))
        refs = refs[4:]
    (own_step_ref, other_step_ref, own_value_ref, other_value_ref, inverse_ref, from_ahead_ref,
     from_back_ref, rest_ref) = refs
    cases, order = own_value_ref.shape
    mine = lax.axis_index("row")
    odd = (mine & 1) == 1
    eye = (
        lax.broadcasted_iota(jnp.int32, (order, order), 0)
        == lax.broadcasted_iota(jnp.int32, (order, order), 1)
    ).astype(f32)
    none, last = jnp.zeros((order, order), f32), jnp.zeros((cases, order), f32)
    ahead = jnp.concatenate([eye, none, last], axis=0)
    back = jnp.concatenate([none, eye, last], axis=0)

    def shifted(value):
        return jnp.concatenate([none, none, value], axis=0)

    for stride, own_maps, other_maps, own_shifts, other_shifts in levels[::-1]:
        upper = (mine & stride) != 0
        first_phi = jnp.where(upper, other_maps[:order, :], own_maps[:order, :])
        second_maps = jnp.where(upper, own_maps[...], other_maps[...])
        own, other = own_shifts[...], other_shifts[...]
        first_shift = jnp.where(upper, other[:cases], own[:cases])
        second_shift = jnp.where(upper, own[cases:], other[cases:])
        middle = dot_rows(ahead, split(first_phi), NT) + shifted(first_shift)
        inner = (
            dot_rows(back, split(second_maps[:order]), NN)
            - dot_rows(middle, split(second_maps[order:]), NN)
            + shifted(second_shift)
        )
        ahead = jnp.where(upper, middle, ahead)
        back = jnp.where(upper, back, inner)

    own_step, other_step = own_step_ref[...], other_step_ref[...]
    own_value, other_value = own_value_ref[...], other_value_ref[...]
    first_step = split(jnp.where(odd, other_step, own_step))
    second_step = split(jnp.where(odd, own_step, other_step))
    first = dot_rows(ahead, first_step, NT) + shifted(jnp.where(odd, other_value, own_value))
    second = dot_rows(first, second_step, NT) + shifted(jnp.where(odd, own_value, other_value))
    inner = dot_rows(back - second, second_step, NN)
    solved = dot_rows(
        jnp.where(odd, second - back, first - inner), split(inverse_ref[...]), NN
    )
    from_ahead_ref[...] = solved[:order]
    from_back_ref[...] = solved[order : 2 * order]
    rest_ref[...] = solved[2 * order :]


def local_call(strides, levels, leaf):
    order = leaf[0].shape[0]
    cases = leaf[2].shape[0]
    square = jax.ShapeDtypeStruct((order, order), f32)
    return pl.pallas_call(
        functools.partial(local_kernel, strides),
        out_shape=[square, square, jax.ShapeDtypeStruct((cases, order), f32)],
        compiler_params=small(6),
        cost_estimate=pl.CostEstimate(flops=10**9, bytes_accessed=10**6, transcendentals=0),
        name="local_solution",
    )(*levels, *leaf)


def finish_kernel(width, ways, *refs):
    own_maps_ref, got_ref, swapped_ref, *refs = refs
    order = own_maps_ref.shape[1]
    shifts, refs = refs[:ways], refs[ways:]
    (from_ahead_ref, from_back_ref, rest_ref, inner_base, outer_base,
     labels_ref,
     weight_ref, updated_hbm, solution_hbm, all_maps, all_shifts, ahead_ref, back_ref, updated,
     solution, out_sems) = refs
    cases = rest_ref.shape[0]
    comps, layers, section = labels_ref.shape
    mine = lax.axis_index("row")
    odd = (mine & 1) == 1
    group = mine // width

    all_maps[group] = own_maps_ref[...]
    for hop in range(1, ways):
        part = slice((hop - 1) * order, hop * order)
        got, swapped = got_ref[part, :], swapped_ref[part, :]
        all_maps[group ^ hop, :order] = jnp.where(odd, swapped, got)
        all_maps[group ^ hop, order:] = jnp.where(odd, got, swapped)
    for hop in range(ways):
        all_shifts[group ^ hop_order[hop]] = shifts[hop][...]

    ahead = all_shifts[0, :cases]
    ahead_ref[0] = jnp.zeros_like(ahead)
    ahead_ref[1] = ahead
    for at in range(1, ways - 1):
        ahead = dot_rows(ahead, split(all_maps[at, :order]), NT) + all_shifts[at, :cases]
        ahead_ref[at + 1] = ahead
    back = jnp.zeros_like(ahead)
    back_ref[ways - 1] = back
    for at in range(ways - 1, 0, -1):
        own = all_shifts[at, cases:] - dot_rows(ahead_ref[at], split(all_maps[at, order:]), NN)
        last = at == ways - 1
        back = own if last else own + dot_rows(back, split(all_maps[at, :order]), NN)
        back_ref[at - 1] = back
    ahead, back = ahead_ref[group], back_ref[group]

    solved = (
        dot_rows(ahead, split(from_ahead_ref[...]), NN)
        + dot_rows(back, split(from_back_ref[...]), NN)
        + rest_ref[...]
    )
    solution[...] = solved
    out_copies = [pltpu.make_async_copy(solution, solution_hbm, out_sems.at[comps])]
    out_copies[0].start()

    for comp in range(comps):
        for tile in range(section // 128):
            lanes = slice(tile * 128, (tile + 1) * 128)
            label = labels_ref[comp, :, lanes]
            weight = weight_ref[comp, :, lanes]
            for case in range(cases):
                table = jnp.broadcast_to(solved[case : case + 1, :], (layers, 128))
                spread = jnp.take_along_axis(table, label, axis=1, mode="promise_in_bounds")
                correction = weight * spread
                middle = slice(8, layers - 8)
                updated[case, comp, middle, lanes] = (
                    inner_base[case, comp, :, lanes] + correction[8 : layers - 8]
                )
                updated[case, comp, :8, lanes] = outer_base[case, comp, :8, lanes] + correction[:8]
                updated[case, comp, layers - 8 :, lanes] = (
                    outer_base[case, comp, 8:, lanes] + correction[layers - 8 :]
                )
        copy = pltpu.make_async_copy(
            updated.at[:, comp], updated_hbm.at[:, comp], out_sems.at[comp]
        )
        copy.start()
        out_copies.append(copy)
    for copy in out_copies:
        copy.wait()


def finish_call(width, maps, shifts, local_maps, inner, outer, labels, weight):
    cases, comps, _, section = inner.shape
    layers = labels.shape[1]
    whole = (cases, comps, layers, section)
    order = maps[0].shape[1]
    ways = len(shifts)
    hbm, local = pl.BlockSpec(memory_space=pltpu.HBM), pl.BlockSpec(memory_space=pltpu.VMEM)
    before = (*maps, *[shifts[hop] for hop in hop_order], *local_maps)
    return pl.pallas_call(
        functools.partial(finish_kernel, width, ways),
        in_specs=[local] * (len(before) + 4),
        out_specs=[hbm, hbm],
        out_shape=[
            jax.ShapeDtypeStruct(whole, f32),
            jax.ShapeDtypeStruct((cases, order), f32),
        ],
        scratch_shapes=[
            pltpu.VMEM((ways, 2 * order, order), f32),
            pltpu.VMEM((ways, 2 * cases, order), f32),
            pltpu.VMEM((ways, cases, order), f32),
            pltpu.VMEM((ways, cases, order), f32),
            pltpu.VMEM(whole, f32),
            pltpu.VMEM((cases, order), f32),
            pltpu.SemaphoreType.DMA((comps + 1,)),
        ],
        compiler_params=small(10),
        name="finish",
    )(*before, inner, outer, labels, weight)


def per_device(
    displacement, loads, section_stiffness, modulus, aggregate, basis_weight, diag_inverse, sub_factor
):
    count = lax.axis_size("row")
    ways = 4
    width = count // ways

    def swap(value, mask):
        return lax.ppermute(value, "row", [(i, i ^ mask) for i in range(count)])

    step, near, far = start_call(diag_inverse, sub_factor, displacement)
    other_step = swap(step, 1)
    near = swap(near, 1)
    far = lax.ppermute(
        far, "row", [(i, i + 1 if i & 1 else i - 1) for i in range(1, count - 1)]
    )
    cases, comps, layers, section = displacement.shape
    order = diag_inverse.shape[0]
    outer = (comps, cases, 16, section)
    node_values = (modulus, aggregate, basis_weight)
    inner_base, outer_across, diagonal, total = residual_call(
        inner_kernel,
        False,
        [
            (cases, comps, layers - 16, section),
            outer,
            (comps, 8, section),
            (4 * cases, order // 2),
        ],
        [pltpu.VMEM((comps, cases, layers - 16, section), f32)],
        displacement, loads, section_stiffness, *node_values,
    )
    maps, mixed = maps_call(pair_maps_kernel, "pair_maps", 1, step, other_step)
    pair_operands = (step, other_step, maps, mixed)
    strides, joins = [], []
    stride = 2
    while stride < width:
        other_maps = swap(maps, stride)
        if not strides:
            other_maps, total = lax.optimization_barrier((other_maps, total))
        joined, mixed, half = maps_call(
            functools.partial(join_maps_kernel, stride), "join_maps", 2, maps, other_maps
        )
        strides.append(stride)
        joins.append((maps, other_maps, mixed))
        maps = joined
        stride *= 2
    halves = [swap(half, hop * width) for hop in range(1, ways)]
    outer_base, value = residual_call(
        outer_kernel,
        True,
        [(cases, comps, 16, section), (cases, order)],
        [],
        displacement, loads, *node_values, diag_inverse, near, far, outer_across, diagonal, total,
    )
    other_value = swap(value, 1)
    shifts = shifts_call(pair_shifts_kernel, "pair_shifts", cases, value, other_value, *pair_operands)
    levels = []
    for stride, (own_maps, other_maps, mixed) in zip(strides, joins):
        other_shifts = swap(shifts, stride)
        levels += [own_maps, other_maps, shifts, other_shifts]
        shifts = shifts_call(
            functools.partial(join_shifts_kernel, stride), "join_shifts", cases,
            shifts, other_shifts, own_maps, other_maps, mixed,
        )
    gathered = jnp.concatenate(lax.optimization_barrier((shifts, *halves))[1:], axis=0)
    all_maps = [maps, gathered, swap(gathered, 1)]
    all_shifts = [shifts] + [swap(shifts, hop * width) for hop in range(1, ways)]
    leaf = (step, other_step, value, other_value, diag_inverse)
    local_maps = local_call(tuple(strides), levels, leaf)
    updated, solution_rows = finish_call(
        width, all_maps, all_shifts, local_maps, inner_base, outer_base, aggregate, basis_weight
    )
    return updated, solution_rows.T


def solution(mesh):
    placed = (
        P("groups", None, "row", None),
        P("groups", None, "row", None),
        P("groups", None, None),
        P("row", "groups"),
        P("groups", "row", None),
        P("groups", "row", None),
        P("row", "groups"),
        P("row", "groups"),
    )
    return jax.shard_map(
        per_device,
        mesh=mesh,
        in_specs=placed,
        out_specs=(P("groups", None, "row", None), P("row", "groups")),
        check_vma=False,
    )
```

```python
import functools

import jax
import jax.numpy as jnp
from jax import lax
from jax.experimental import pallas as pl
from jax.experimental.pallas import tpu as pltpu
from jax.sharding import PartitionSpec as P

span_weights = (1.5, -0.15, 1.0 / 90.0)
hop_order = (0, 1, 3, 2)
bf16, f32 = jnp.bfloat16, jnp.float32
NN = (((1,), (0,)), ((), ()))
NT = (((1,), (1,)), ((), ()))
TN = (((0,), (0,)), ((), ()))


def split(value):
    high = value.astype(bf16)
    return high, (value - high.astype(f32)).astype(bf16)


def dot(left, right, dims):
    return lax.dot_general(left, right, dims, preferred_element_type=f32)


def dot3(left, right, dims):
    left_high, left_low = left
    right_high, right_low = right
    return dot(left_high, right_high, dims) + (
        dot(left_high, right_low, dims) + dot(left_low, right_high, dims)
    )


def dot_rows(rows, weights, dims):
    high, low = split(rows)
    count = rows.shape[0]
    left = jnp.concatenate(
        [
            jnp.concatenate([high, high], axis=1),
            jnp.concatenate([low, jnp.zeros_like(low)], axis=1),
        ],
        axis=0,
    )
    both = dot(left, jnp.concatenate(weights, axis=dims[0][1][0]), dims)
    return both[:count] + both[count:]


def node_rows(edge, layers):
    return (0, layers - 8) if edge else tuple(range(8, layers - 8, 8))


def residual_part(
    edge, disp_ref, loads_ref, modulus_ref, labels_ref, weight_ref, across_ref, diagonal_of, padded,
    weighted, base_ref, comp, total,
):
    cases, comps, layers, section = disp_ref.shape
    tiles = section // 128
    groups = node_rows(edge, layers)
    depth = 8 * len(groups)
    stride = weighted.shape[1] // cases
    fine = total.shape[1]
    parts = total.shape[0] // (2 * cases)
    bins = lax.broadcasted_iota(jnp.int32, (fine, 128), 0).astype(f32).astype(bf16)
    for at, first in enumerate(groups):
        rows = slice(first, first + 8)
        out = slice(at * 8, at * 8 + 8)
        for tile in range(tiles):
            lanes = slice(tile * 128, (tile + 1) * 128)
            modulus = modulus_ref[rows, lanes]
            diagonal = diagonal_of(comp, lanes)
            inverse = 1.0 / (modulus * (2.0 * sum(span_weights)) + diagonal)
            weight = weight_ref[comp, rows, lanes]
            for case in range(cases):
                own = padded[comp, case, tile, 8 + first : 16 + first, :]
                span_sum = (2.0 * sum(span_weights)) * own
                for offset in range(1, 4):
                    low = padded[comp, case, tile, 8 + first - offset : 16 + first - offset, :]
                    high = padded[comp, case, tile, 8 + first + offset : 16 + first + offset, :]
                    span_sum = span_sum - span_weights[offset - 1] * (low + high)
                residual = loads_ref[case, comp, rows, lanes] - (
                    modulus * span_sum + across_ref[comp, case, out, lanes]
                )
                base_ref[case, comp, out, lanes] = own + residual * inverse
                start = case * stride + tile * depth + at * 8
                weighted[comp, start : start + 8, :] = weight * residual

    def restrict(group, total):
        at = pl.multiple_of(group * 8, 8)
        first = pl.multiple_of(groups[0] + group * (groups[1] - groups[0]), 8)
        block = labels_ref[comp, pl.ds(first, 8), :]
        big = lax.shift_right_logical(block, fine.bit_length() - 1).astype(f32)
        little = (block & (fine - 1)).astype(f32)
        for inner in range(8):
            onehots, values = [], []
            for tile in range(tiles):
                lanes = slice(tile * 128, (tile + 1) * 128)
                low = jnp.broadcast_to(little[inner : inner + 1, lanes], (16, 128)).astype(bf16)
                low = jnp.concatenate([low] * (fine // 16), axis=0)
                onehots.append(jnp.where(low == bins, bf16(1), bf16(0)))
                high = jnp.broadcast_to(big[inner : inner + 1, lanes], (16, 128)).astype(bf16)
                value = weighted[comp, pl.ds(tile * depth + at + inner, cases, stride=stride), :]
                value = jnp.concatenate(split(value), axis=0)
                values.append(
                    jnp.concatenate(
                        [jnp.where(high == bf16(part), value, bf16(0)) for part in range(parts)],
                        axis=0,
                    )
                )
            total = total + dot(
                jnp.concatenate(values, axis=1), jnp.concatenate(onehots, axis=1), NT
            )
        return total

    return lax.fori_loop(0, len(groups), restrict, total)


def inner_kernel(
    disp_ref, loads_ref, section_ref, modulus_ref, labels_ref, weight_ref,
    base_ref, outer_ref, diagonal_ref, total_ref, padded, weighted, across_ref,
):
    cases, comps, layers, section = disp_ref.shape
    tiles = section // 128
    same = lax.broadcasted_iota(jnp.int32, (128, 128), 0) == lax.broadcasted_iota(
        jnp.int32, (128, 128), 1
    )
    total = jnp.zeros(total_ref.shape, f32)
    for comp in range(comps):
        for tile in range(tiles):
            lanes = slice(tile * 128, (tile + 1) * 128)
            padded[comp, :, tile, 8 : 8 + layers, :] = disp_ref[:, comp, :, lanes]
        high, low = split(disp_ref[:, comp].reshape(cases * layers, section))
        section_high, section_low = split(section_ref[comp])
        across = dot(
            jnp.concatenate([high, high, low], axis=1),
            jnp.concatenate([section_high, section_low, section_high], axis=0),
            NN,
        ).reshape(cases, layers, section)
        across_ref[comp] = across[:, 8 : layers - 8]
        outer_ref[comp, :, :8] = across[:, :8]
        outer_ref[comp, :, 8:] = across[:, layers - 8 :]
        diagonals = []
        for tile in range(tiles):
            lanes = slice(tile * 128, (tile + 1) * 128)
            block = section_ref[comp, lanes, lanes]
            diagonals.append(jnp.sum(jnp.where(same, block, 0.0), axis=0, keepdims=True))
            diagonal_ref[comp, :, lanes] = jnp.broadcast_to(diagonals[-1], (8, 128))
        total = residual_part(
            False, disp_ref, loads_ref, modulus_ref, labels_ref, weight_ref, across_ref,
            lambda _, lanes: diagonals[lanes.start // 128], padded, weighted, base_ref, comp, total,
        )
    total_ref[...] = total


def outer_kernel(
    disp_ref, loads_ref, modulus_ref, labels_ref, weight_ref, inverse_ref, near_ref, far_ref,
    across_ref, diagonal_ref, inner_total_ref, base_ref, value_ref, padded, weighted,
):
    cases, comps, layers, section = disp_ref.shape
    mine = lax.axis_index("row")
    odd = (mine & 1) == 1
    lowest, highest = mine == 0, mine == lax.axis_size("row") - 1
    tiles = section // 128
    total = inner_total_ref[...]
    for comp in range(comps):
        for tile in range(tiles):
            lanes = slice(tile * 128, (tile + 1) * 128)
            padded[comp, :, tile, 8:24, :] = disp_ref[:, comp, :16, lanes]
            padded[comp, :, tile, layers - 8 : layers + 8, :] = disp_ref[
                :, comp, layers - 16 :, lanes
            ]
            for row in range(3):
                at = (tile * 3 + row) * cases * comps + comp * cases
                near, far = near_ref[at : at + cases, :], far_ref[at : at + cases, :]
                below = jnp.where(lowest, 0.0, jnp.where(odd, near, far))
                above = jnp.where(highest, 0.0, jnp.where(odd, far, near))
                for case in range(cases):
                    padded[comp, case, tile, 5 + row : 6 + row, :] = below[case : case + 1]
                    low = 8 + layers + row
                    padded[comp, case, tile, low : low + 1, :] = above[case : case + 1]
        total = residual_part(
            True, disp_ref, loads_ref, modulus_ref, labels_ref, weight_ref, across_ref,
            lambda comp, lanes: diagonal_ref[comp, :, lanes], padded, weighted, base_ref, comp,
            total,
        )
    sums = []
    for at in range(0, total.shape[0], 2 * cases):
        sums.append(total[at : at + cases] + total[at + cases : at + 2 * cases])
    value_ref[...] = dot_rows(jnp.concatenate(sums, axis=1), split(inverse_ref[...]), NT)


def residual_call(kernel, edge, out_shape, scratch_shapes, *operands):
    cases, comps, layers, section = operands[0].shape
    tiles = section // 128
    depth = 8 * len(node_rows(edge, layers))
    local = pl.BlockSpec(memory_space=pltpu.VMEM)
    return pl.pallas_call(
        kernel,
        in_specs=[local] * len(operands),
        out_specs=[local] * len(out_shape),
        out_shape=[jax.ShapeDtypeStruct(shape, f32) for shape in out_shape],
        scratch_shapes=[
            pltpu.VMEM((comps, cases, tiles, layers + 16, 128), f32),
            pltpu.VMEM((comps, cases * (tiles * depth + 8), 128), f32),
            *scratch_shapes,
        ],
        compiler_params=pltpu.CompilerParams(vmem_limit_bytes=14 << 20),
        cost_estimate=pl.CostEstimate(
            flops=3 * cases * comps * layers * section * section,
            bytes_accessed=8 * operands[0].size,
            transcendentals=0,
        ),
        name="outer_residual" if edge else "inner_residual",
    )(*operands)


def small(limit):
    return pltpu.CompilerParams(vmem_limit_bytes=limit << 20)


def in_hbm(*values):
    return [pltpu.with_memory_space_constraint(value, pltpu.HBM) for value in values]


def start_kernel(
    inverse_hbm, sub_hbm, disp_hbm, step_ref, near_ref, far_ref, inverse, sub, first, last, sems
):
    cases, comps, rows, section = first.shape
    layers = disp_hbm.shape[2]
    copies = [
        pltpu.make_async_copy(inverse_hbm, inverse, sems.at[0]),
        pltpu.make_async_copy(sub_hbm, sub, sems.at[1]),
        pltpu.make_async_copy(disp_hbm.at[:, :, pl.ds(0, rows), :], first, sems.at[2]),
        pltpu.make_async_copy(disp_hbm.at[:, :, pl.ds(layers - rows, rows), :], last, sems.at[3]),
    ]
    for copy in copies:
        copy.start()
    odd = (lax.axis_index("row") & 1) == 1
    copies[0].wait()
    copies[1].wait()
    step_ref[...] = -dot3(split(inverse[...]), split(sub[...]), NN)
    copies[2].wait()
    copies[3].wait()
    for tile in range(section // 128):
        lanes = slice(tile * 128, (tile + 1) * 128)
        for row in range(3):
            for comp in range(comps):
                at = (tile * 3 + row) * cases * comps + comp * cases
                low = first[:, comp, row, lanes]
                high = last[:, comp, rows - 3 + row, lanes]
                near_ref[at : at + cases, :] = jnp.where(odd, low, high)
                far_ref[at : at + cases, :] = jnp.where(odd, high, low)


def start_call(diag_inverse, sub_factor, displacement):
    cases, comps, layers, section = displacement.shape
    packed = jax.ShapeDtypeStruct((cases * comps * 3 * section // 128, 128), f32)
    block = pltpu.VMEM((cases, comps, 8, section), f32)
    square = pltpu.VMEM(diag_inverse.shape, f32)
    return pl.pallas_call(
        start_kernel,
        in_specs=[pl.BlockSpec(memory_space=pltpu.HBM)] * 3,
        out_specs=[pl.BlockSpec(memory_space=pltpu.VMEM)] * 3,
        out_shape=[jax.ShapeDtypeStruct(diag_inverse.shape, f32), packed, packed],
        scratch_shapes=[square, square, block, block, pltpu.SemaphoreType.DMA((4,))],
        compiler_params=small(4),
        cost_estimate=pl.CostEstimate(flops=10**10, bytes_accessed=10**6, transcendentals=0),
        name="start",
    )(*in_hbm(diag_inverse, sub_factor, displacement))


def pair_maps_kernel(own_ref, other_ref, maps_ref, mixed_ref):
    order = own_ref.shape[0]
    odd = (lax.axis_index("row") & 1) == 1
    own, other = own_ref[...], other_ref[...]
    first = jnp.where(odd, other, own)
    first_split, second_split = split(first), split(jnp.where(odd, own, other))
    phi = dot3(second_split, first_split, NN)
    phi_split = split(phi)
    gram = dot3(first_split, first_split, TN) + dot3(phi_split, phi_split, TN)
    maps_ref[:order, :] = phi
    maps_ref[order:, :] = gram
    mixed_ref[...] = first + dot3(second_split, phi_split, TN)


def join_maps_kernel(stride, own_ref, other_ref, maps_ref, mixed_ref, half_ref):
    order = own_ref.shape[1]
    upper = (lax.axis_index("row") & stride) != 0
    own, other = own_ref[...], other_ref[...]
    first, second = jnp.where(upper, other, own), jnp.where(upper, own, other)
    first_phi = split(first[:order])
    mixed = dot3(split(second[order:]), first_phi, NN)
    phi = dot3(split(second[:order]), first_phi, NN)
    gram = first[order:] + dot3(first_phi, split(mixed), TN)
    maps_ref[:order, :] = phi
    maps_ref[order:, :] = gram
    mixed_ref[...] = mixed
    odd = (lax.axis_index("row") & 1) == 1
    half_ref[...] = jnp.where(odd, gram, phi)


def maps_call(kernel, name, extra, own, other):
    order = own.shape[1]
    return pl.pallas_call(
        kernel,
        out_shape=[
            jax.ShapeDtypeStruct((2 * order, order), f32),
        ]
        + [jax.ShapeDtypeStruct((order, order), f32)] * extra,
        compiler_params=small(3),
        cost_estimate=pl.CostEstimate(flops=10**10, bytes_accessed=10**6, transcendentals=0),
        name=name,
    )(own, other)


def pair_shifts_kernel(own_ref, other_ref, own_step_ref, other_step_ref, maps_ref, mixed_ref, out_ref):
    cases, order = own_ref.shape
    odd = (lax.axis_index("row") & 1) == 1
    own, other = own_ref[...], other_ref[...]
    first, second = jnp.where(odd, other, own), jnp.where(odd, own, other)
    second_step = jnp.where(odd, own_step_ref[...], other_step_ref[...])
    out_ref[:cases, :] = dot_rows(first, split(second_step), NT) + second
    out_ref[cases:, :] = -(
        dot_rows(first, split(mixed_ref[...]), NN)
        + dot_rows(second, split(maps_ref[:order, :]), NN)
    )


def join_shifts_kernel(stride, own_ref, other_ref, own_maps_ref, other_maps_ref, mixed_ref, out_ref):
    order = mixed_ref.shape[0]
    cases = own_ref.shape[0] // 2
    upper = (lax.axis_index("row") & stride) != 0
    own, other = own_ref[...], other_ref[...]
    first, second = jnp.where(upper, other, own), jnp.where(upper, own, other)
    own_phi, other_phi = own_maps_ref[:order, :], other_maps_ref[:order, :]
    first_phi = jnp.where(upper, other_phi, own_phi)
    second_phi = jnp.where(upper, own_phi, other_phi)
    out_ref[:cases, :] = dot_rows(first[:cases], split(second_phi), NT) + second[:cases]
    out_ref[cases:, :] = (
        first[cases:]
        + dot_rows(second[cases:], split(first_phi), NN)
        - dot_rows(first[:cases], split(mixed_ref[...]), NN)
    )


def shifts_call(kernel, name, cases, *operands):
    return pl.pallas_call(
        kernel,
        out_shape=jax.ShapeDtypeStruct((2 * cases, operands[0].shape[1]), f32),
        compiler_params=small(3),
        name=name,
    )(*operands)


def local_kernel(strides, *refs):
    levels = []
    for stride in strides:
        levels.append((stride, *refs[:4]))
        refs = refs[4:]
    (own_step_ref, other_step_ref, own_value_ref, other_value_ref, inverse_ref, from_ahead_ref,
     from_back_ref, rest_ref) = refs
    cases, order = own_value_ref.shape
    mine = lax.axis_index("row")
    odd = (mine & 1) == 1
    eye = (
        lax.broadcasted_iota(jnp.int32, (order, order), 0)
        == lax.broadcasted_iota(jnp.int32, (order, order), 1)
    ).astype(f32)
    none, last = jnp.zeros((order, order), f32), jnp.zeros((cases, order), f32)
    ahead = jnp.concatenate([eye, none, last], axis=0)
    back = jnp.concatenate([none, eye, last], axis=0)

    def shifted(value):
        return jnp.concatenate([none, none, value], axis=0)

    for stride, own_maps, other_maps, own_shifts, other_shifts in levels[::-1]:
        upper = (mine & stride) != 0
        first_phi = jnp.where(upper, other_maps[:order, :], own_maps[:order, :])
        second_maps = jnp.where(upper, own_maps[...], other_maps[...])
        own, other = own_shifts[...], other_shifts[...]
        first_shift = jnp.where(upper, other[:cases], own[:cases])
        second_shift = jnp.where(upper, own[cases:], other[cases:])
        middle = dot_rows(ahead, split(first_phi), NT) + shifted(first_shift)
        inner = (
            dot_rows(back, split(second_maps[:order]), NN)
            - dot_rows(middle, split(second_maps[order:]), NN)
            + shifted(second_shift)
        )
        ahead = jnp.where(upper, middle, ahead)
        back = jnp.where(upper, back, inner)

    own_step, other_step = own_step_ref[...], other_step_ref[...]
    own_value, other_value = own_value_ref[...], other_value_ref[...]
    first_step = split(jnp.where(odd, other_step, own_step))
    second_step = split(jnp.where(odd, own_step, other_step))
    first = dot_rows(ahead, first_step, NT) + shifted(jnp.where(odd, other_value, own_value))
    second = dot_rows(first, second_step, NT) + shifted(jnp.where(odd, own_value, other_value))
    inner = dot_rows(back - second, second_step, NN)
    solved = dot_rows(
        jnp.where(odd, second - back, first - inner), split(inverse_ref[...]), NN
    )
    from_ahead_ref[...] = solved[:order]
    from_back_ref[...] = solved[order : 2 * order]
    rest_ref[...] = solved[2 * order :]


def local_call(strides, levels, leaf):
    order = leaf[0].shape[0]
    cases = leaf[2].shape[0]
    square = jax.ShapeDtypeStruct((order, order), f32)
    return pl.pallas_call(
        functools.partial(local_kernel, strides),
        out_shape=[square, square, jax.ShapeDtypeStruct((cases, order), f32)],
        compiler_params=small(6),
        cost_estimate=pl.CostEstimate(flops=10**9, bytes_accessed=10**6, transcendentals=0),
        name="local_solution",
    )(*levels, *leaf)


def finish_kernel(width, ways, *refs):
    own_maps_ref, got_ref, swapped_ref, *refs = refs
    order = own_maps_ref.shape[1]
    shifts, refs = refs[:ways], refs[ways:]
    (from_ahead_ref, from_back_ref, rest_ref, inner_base, outer_base,
     labels_ref,
     weight_ref, updated_hbm, solution_hbm, all_maps, all_shifts, ahead_ref, back_ref, updated,
     solution, out_sems) = refs
    cases = rest_ref.shape[0]
    comps, layers, section = labels_ref.shape
    mine = lax.axis_index("row")
    odd = (mine & 1) == 1
    group = mine // width

    all_maps[group] = own_maps_ref[...]
    for hop in range(1, ways):
        part = slice((hop - 1) * order, hop * order)
        got, swapped = got_ref[part, :], swapped_ref[part, :]
        all_maps[group ^ hop, :order] = jnp.where(odd, got, swapped)
        all_maps[group ^ hop, order:] = jnp.where(odd, swapped, got)
    for hop in range(ways):
        all_shifts[group ^ hop_order[hop]] = shifts[hop][...]

    ahead = all_shifts[0, :cases]
    ahead_ref[0] = jnp.zeros_like(ahead)
    ahead_ref[1] = ahead
    for at in range(1, ways - 1):
        ahead = dot_rows(ahead, split(all_maps[at, :order]), NT) + all_shifts[at, :cases]
        ahead_ref[at + 1] = ahead
    back = jnp.zeros_like(ahead)
    back_ref[ways - 1] = back
    for at in range(ways - 1, 0, -1):
        own = all_shifts[at, cases:] - dot_rows(ahead_ref[at], split(all_maps[at, order:]), NN)
        last = at == ways - 1
        back = own if last else own + dot_rows(back, split(all_maps[at, :order]), NN)
        back_ref[at - 1] = back
    ahead, back = ahead_ref[group], back_ref[group]

    solved = (
        dot_rows(ahead, split(from_ahead_ref[...]), NN)
        + dot_rows(back, split(from_back_ref[...]), NN)
        + rest_ref[...]
    )
    solution[...] = solved
    out_copies = [pltpu.make_async_copy(solution, solution_hbm, out_sems.at[comps])]
    out_copies[0].start()

    for comp in range(comps):
        for tile in range(section // 128):
            lanes = slice(tile * 128, (tile + 1) * 128)
            label = labels_ref[comp, :, lanes]
            weight = weight_ref[comp, :, lanes]
            for case in range(cases):
                table = jnp.broadcast_to(solved[case : case + 1, :], (layers, 128))
                spread = jnp.take_along_axis(table, label, axis=1, mode="promise_in_bounds")
                correction = weight * spread
                middle = slice(8, layers - 8)
                updated[case, comp, middle, lanes] = (
                    inner_base[case, comp, :, lanes] + correction[8 : layers - 8]
                )
                updated[case, comp, :8, lanes] = outer_base[case, comp, :8, lanes] + correction[:8]
                updated[case, comp, layers - 8 :, lanes] = (
                    outer_base[case, comp, 8:, lanes] + correction[layers - 8 :]
                )
        copy = pltpu.make_async_copy(
            updated.at[:, comp], updated_hbm.at[:, comp], out_sems.at[comp]
        )
        copy.start()
        out_copies.append(copy)
    for copy in out_copies:
        copy.wait()


def finish_call(width, maps, shifts, local_maps, inner, outer, labels, weight):
    cases, comps, _, section = inner.shape
    layers = labels.shape[1]
    whole = (cases, comps, layers, section)
    order = maps[0].shape[1]
    ways = len(shifts)
    hbm, local = pl.BlockSpec(memory_space=pltpu.HBM), pl.BlockSpec(memory_space=pltpu.VMEM)
    before = (*maps, *[shifts[hop] for hop in hop_order], *local_maps)
    return pl.pallas_call(
        functools.partial(finish_kernel, width, ways),
        in_specs=[local] * (len(before) + 4),
        out_specs=[hbm, hbm],
        out_shape=[
            jax.ShapeDtypeStruct(whole, f32),
            jax.ShapeDtypeStruct((cases, order), f32),
        ],
        scratch_shapes=[
            pltpu.VMEM((ways, 2 * order, order), f32),
            pltpu.VMEM((ways, 2 * cases, order), f32),
            pltpu.VMEM((ways, cases, order), f32),
            pltpu.VMEM((ways, cases, order), f32),
            pltpu.VMEM(whole, f32),
            pltpu.VMEM((cases, order), f32),
            pltpu.SemaphoreType.DMA((comps + 1,)),
        ],
        compiler_params=small(10),
        name="finish",
    )(*before, inner, outer, labels, weight)


def per_device(
    displacement, loads, section_stiffness, modulus, aggregate, basis_weight, diag_inverse, sub_factor
):
    count = lax.axis_size("row")
    ways = 4
    width = count // ways

    def swap(value, mask):
        return lax.ppermute(value, "row", [(i, i ^ mask) for i in range(count)])

    step, near, far = start_call(diag_inverse, sub_factor, displacement)
    other_step = swap(step, 1)
    near = swap(near, 1)
    far = lax.ppermute(
        far, "row", [(i, i + 1 if i & 1 else i - 1) for i in range(1, count - 1)]
    )
    cases, comps, layers, section = displacement.shape
    order = diag_inverse.shape[0]
    outer = (comps, cases, 16, section)
    node_values = (modulus, aggregate, basis_weight)
    inner_base, outer_across, diagonal, total = residual_call(
        inner_kernel,
        False,
        [
            (cases, comps, layers - 16, section),
            outer,
            (comps, 8, section),
            (4 * cases, order // 2),
        ],
        [pltpu.VMEM((comps, cases, layers - 16, section), f32)],
        displacement, loads, section_stiffness, *node_values,
    )
    maps, mixed = maps_call(pair_maps_kernel, "pair_maps", 1, step, other_step)
    pair_operands = (step, other_step, maps, mixed)
    strides, joins = [], []
    stride = 2
    while stride < width:
        other_maps = swap(maps, stride ^ 1)
        if not strides:
            other_maps, total = lax.optimization_barrier((other_maps, total))
        joined, mixed, half = maps_call(
            functools.partial(join_maps_kernel, stride), "join_maps", 2, maps, other_maps
        )
        strides.append(stride)
        joins.append((maps, other_maps, mixed))
        maps = joined
        stride *= 2
    halves = [swap(half, hop * width ^ 1) for hop in range(1, ways)]
    outer_base, value = residual_call(
        outer_kernel,
        True,
        [(cases, comps, 16, section), (cases, order)],
        [],
        displacement, loads, *node_values, diag_inverse, near, far, outer_across, diagonal, total,
    )
    other_value = swap(value, 1)
    shifts = shifts_call(pair_shifts_kernel, "pair_shifts", cases, value, other_value, *pair_operands)
    levels = []
    for stride, (own_maps, other_maps, mixed) in zip(strides, joins):
        other_shifts = swap(shifts, stride ^ 1)
        levels += [own_maps, other_maps, shifts, other_shifts]
        shifts = shifts_call(
            functools.partial(join_shifts_kernel, stride), "join_shifts", cases,
            shifts, other_shifts, own_maps, other_maps, mixed,
        )
    gathered = jnp.concatenate(lax.optimization_barrier((shifts, *halves))[1:], axis=0)
    all_maps = [maps, gathered, swap(gathered, 1)]
    all_shifts = [shifts] + [swap(shifts, hop * width ^ 1) for hop in range(1, ways)]
    leaf = (step, other_step, value, other_value, diag_inverse)
    local_maps = local_call(tuple(strides), levels, leaf)
    updated, solution_rows = finish_call(
        width, all_maps, all_shifts, local_maps, inner_base, outer_base, aggregate, basis_weight
    )
    return updated, solution_rows.T


def solution(mesh):
    placed = (
        P("groups", None, "row", None),
        P("groups", None, "row", None),
        P("groups", None, None),
        P("row", "groups"),
        P("groups", "row", None),
        P("groups", "row", None),
        P("row", "groups"),
        P("row", "groups"),
    )
    return jax.shard_map(
        per_device,
        mesh=mesh,
        in_specs=placed,
        out_specs=(P("groups", None, "row", None), P("row", "groups")),
        check_vma=False,
    )
```

```python
import functools

import jax
import jax.numpy as jnp
from jax import lax
from jax.experimental import pallas as pl
from jax.experimental.pallas import tpu as pltpu
from jax.sharding import PartitionSpec as P

span_weights = (1.5, -0.15, 1.0 / 90.0)
hop_order = (0, 1, 3, 2)
bf16, f32 = jnp.bfloat16, jnp.float32
NN = (((1,), (0,)), ((), ()))
NT = (((1,), (1,)), ((), ()))
TN = (((0,), (0,)), ((), ()))


def split(value):
    high = value.astype(bf16)
    return high, (value - high.astype(f32)).astype(bf16)


def dot(left, right, dims):
    return lax.dot_general(left, right, dims, preferred_element_type=f32)


def dot3(left, right, dims):
    left_high, left_low = left
    right_high, right_low = right
    return dot(left_high, right_high, dims) + (
        dot(left_high, right_low, dims) + dot(left_low, right_high, dims)
    )


def dot_rows(rows, weights, dims):
    high, low = split(rows)
    count = rows.shape[0]
    left = jnp.concatenate(
        [
            jnp.concatenate([high, high], axis=1),
            jnp.concatenate([low, jnp.zeros_like(low)], axis=1),
        ],
        axis=0,
    )
    both = dot(left, jnp.concatenate(weights, axis=dims[0][1][0]), dims)
    return both[:count] + both[count:]


def node_rows(edge, layers):
    return (0, layers - 8) if edge else tuple(range(8, layers - 8, 8))


def residual_part(
    edge, disp_ref, loads_ref, modulus_ref, labels_ref, weight_ref, across_ref, diagonal_of, padded,
    weighted, base_ref, comp, total,
):
    cases, comps, layers, section = disp_ref.shape
    tiles = section // 128
    groups = node_rows(edge, layers)
    depth = 8 * len(groups)
    stride = weighted.shape[1] // cases
    fine = total.shape[1]
    parts = total.shape[0] // (2 * cases)
    bins = lax.broadcasted_iota(jnp.int32, (fine, 128), 0).astype(f32).astype(bf16)
    for at, first in enumerate(groups):
        rows = slice(first, first + 8)
        out = slice(at * 8, at * 8 + 8)
        for tile in range(tiles):
            lanes = slice(tile * 128, (tile + 1) * 128)
            modulus = modulus_ref[rows, lanes]
            diagonal = diagonal_of(comp, lanes)
            inverse = 1.0 / (modulus * (2.0 * sum(span_weights)) + diagonal)
            weight = weight_ref[comp, rows, lanes]
            for case in range(cases):
                own = padded[comp, case, tile, 8 + first : 16 + first, :]
                span_sum = (2.0 * sum(span_weights)) * own
                for offset in range(1, 4):
                    low = padded[comp, case, tile, 8 + first - offset : 16 + first - offset, :]
                    high = padded[comp, case, tile, 8 + first + offset : 16 + first + offset, :]
                    span_sum = span_sum - span_weights[offset - 1] * (low + high)
                residual = loads_ref[case, comp, rows, lanes] - (
                    modulus * span_sum + across_ref[comp, case, out, lanes]
                )
                base_ref[case, comp, out, lanes] = own + residual * inverse
                start = case * stride + tile * depth + at * 8
                weighted[comp, start : start + 8, :] = weight * residual

    def restrict(group, total):
        at = pl.multiple_of(group * 8, 8)
        first = pl.multiple_of(groups[0] + group * (groups[1] - groups[0]), 8)
        block = labels_ref[comp, pl.ds(first, 8), :]
        big = lax.shift_right_logical(block, fine.bit_length() - 1).astype(f32)
        little = (block & (fine - 1)).astype(f32)
        for inner in range(8):
            onehots, values = [], []
            for tile in range(tiles):
                lanes = slice(tile * 128, (tile + 1) * 128)
                low = jnp.broadcast_to(little[inner : inner + 1, lanes], (16, 128)).astype(bf16)
                low = jnp.concatenate([low] * (fine // 16), axis=0)
                onehots.append(jnp.where(low == bins, bf16(1), bf16(0)))
                high = jnp.broadcast_to(big[inner : inner + 1, lanes], (16, 128)).astype(bf16)
                value = weighted[comp, pl.ds(tile * depth + at + inner, cases, stride=stride), :]
                value = jnp.concatenate(split(value), axis=0)
                values.append(
                    jnp.concatenate(
                        [jnp.where(high == bf16(part), value, bf16(0)) for part in range(parts)],
                        axis=0,
                    )
                )
            total = total + dot(
                jnp.concatenate(values, axis=1), jnp.concatenate(onehots, axis=1), NT
            )
        return total

    return lax.fori_loop(0, len(groups), restrict, total)


def inner_kernel(
    disp_ref, loads_ref, section_ref, modulus_ref, labels_ref, weight_ref,
    base_ref, outer_ref, diagonal_ref, total_ref, padded, weighted, across_ref,
):
    cases, comps, layers, section = disp_ref.shape
    tiles = section // 128
    same = lax.broadcasted_iota(jnp.int32, (128, 128), 0) == lax.broadcasted_iota(
        jnp.int32, (128, 128), 1
    )
    total = jnp.zeros(total_ref.shape, f32)
    for comp in range(comps):
        for tile in range(tiles):
            lanes = slice(tile * 128, (tile + 1) * 128)
            padded[comp, :, tile, 8 : 8 + layers, :] = disp_ref[:, comp, :, lanes]
        high, low = split(disp_ref[:, comp].reshape(cases * layers, section))
        section_high, section_low = split(section_ref[comp])
        across = dot(
            jnp.concatenate([high, high, low], axis=1),
            jnp.concatenate([section_high, section_low, section_high], axis=0),
            NN,
        ).reshape(cases, layers, section)
        across_ref[comp] = across[:, 8 : layers - 8]
        outer_ref[comp, :, :8] = across[:, :8]
        outer_ref[comp, :, 8:] = across[:, layers - 8 :]
        diagonals = []
        for tile in range(tiles):
            lanes = slice(tile * 128, (tile + 1) * 128)
            block = section_ref[comp, lanes, lanes]
            diagonals.append(jnp.sum(jnp.where(same, block, 0.0), axis=0, keepdims=True))
            diagonal_ref[comp, :, lanes] = jnp.broadcast_to(diagonals[-1], (8, 128))
        total = residual_part(
            False, disp_ref, loads_ref, modulus_ref, labels_ref, weight_ref, across_ref,
            lambda _, lanes: diagonals[lanes.start // 128], padded, weighted, base_ref, comp, total,
        )
    total_ref[...] = total


def outer_kernel(
    disp_ref, loads_ref, modulus_ref, labels_ref, weight_ref, inverse_ref, near_ref, far_ref,
    across_ref, diagonal_ref, inner_total_ref, base_ref, value_ref, padded, weighted,
):
    cases, comps, layers, section = disp_ref.shape
    mine = lax.axis_index("row")
    odd = (mine & 1) == 1
    lowest, highest = mine == 0, mine == lax.axis_size("row") - 1
    tiles = section // 128
    total = inner_total_ref[...]
    for comp in range(comps):
        for tile in range(tiles):
            lanes = slice(tile * 128, (tile + 1) * 128)
            padded[comp, :, tile, 8:24, :] = disp_ref[:, comp, :16, lanes]
            padded[comp, :, tile, layers - 8 : layers + 8, :] = disp_ref[
                :, comp, layers - 16 :, lanes
            ]
            for row in range(3):
                at = (tile * 3 + row) * cases * comps + comp * cases
                near, far = near_ref[at : at + cases, :], far_ref[at : at + cases, :]
                below = jnp.where(lowest, 0.0, jnp.where(odd, near, far))
                above = jnp.where(highest, 0.0, jnp.where(odd, far, near))
                for case in range(cases):
                    padded[comp, case, tile, 5 + row : 6 + row, :] = below[case : case + 1]
                    low = 8 + layers + row
                    padded[comp, case, tile, low : low + 1, :] = above[case : case + 1]
        total = residual_part(
            True, disp_ref, loads_ref, modulus_ref, labels_ref, weight_ref, across_ref,
            lambda comp, lanes: diagonal_ref[comp, :, lanes], padded, weighted, base_ref, comp,
            total,
        )
    sums = []
    for at in range(0, total.shape[0], 2 * cases):
        sums.append(total[at : at + cases] + total[at + cases : at + 2 * cases])
    value_ref[...] = dot_rows(jnp.concatenate(sums, axis=1), split(inverse_ref[...]), NT)


def residual_call(kernel, edge, out_shape, scratch_shapes, *operands):
    cases, comps, layers, section = operands[0].shape
    tiles = section // 128
    depth = 8 * len(node_rows(edge, layers))
    local = pl.BlockSpec(memory_space=pltpu.VMEM)
    return pl.pallas_call(
        kernel,
        in_specs=[local] * len(operands),
        out_specs=[local] * len(out_shape),
        out_shape=[jax.ShapeDtypeStruct(shape, f32) for shape in out_shape],
        scratch_shapes=[
            pltpu.VMEM((comps, cases, tiles, layers + 16, 128), f32),
            pltpu.VMEM((comps, cases * (tiles * depth + 8), 128), f32),
            *scratch_shapes,
        ],
        compiler_params=pltpu.CompilerParams(vmem_limit_bytes=14 << 20),
        cost_estimate=pl.CostEstimate(
            flops=3 * cases * comps * layers * section * section,
            bytes_accessed=8 * operands[0].size,
            transcendentals=0,
        ),
        name="outer_residual" if edge else "inner_residual",
    )(*operands)


def small(limit):
    return pltpu.CompilerParams(vmem_limit_bytes=limit << 20)


def in_hbm(*values):
    return [pltpu.with_memory_space_constraint(value, pltpu.HBM) for value in values]


def start_kernel(
    inverse_hbm, sub_hbm, disp_hbm, step_ref, near_ref, far_ref, inverse, sub, first, last, sems
):
    cases, comps, rows, section = first.shape
    layers = disp_hbm.shape[2]
    copies = [
        pltpu.make_async_copy(inverse_hbm, inverse, sems.at[0]),
        pltpu.make_async_copy(sub_hbm, sub, sems.at[1]),
        pltpu.make_async_copy(disp_hbm.at[:, :, pl.ds(0, rows), :], first, sems.at[2]),
        pltpu.make_async_copy(disp_hbm.at[:, :, pl.ds(layers - rows, rows), :], last, sems.at[3]),
    ]
    for copy in copies:
        copy.start()
    odd = (lax.axis_index("row") & 1) == 1
    copies[0].wait()
    copies[1].wait()
    step_ref[...] = -dot3(split(inverse[...]), split(sub[...]), NN)
    copies[2].wait()
    copies[3].wait()
    for tile in range(section // 128):
        lanes = slice(tile * 128, (tile + 1) * 128)
        for row in range(3):
            for comp in range(comps):
                at = (tile * 3 + row) * cases * comps + comp * cases
                low = first[:, comp, row, lanes]
                high = last[:, comp, rows - 3 + row, lanes]
                near_ref[at : at + cases, :] = jnp.where(odd, low, high)
                far_ref[at : at + cases, :] = jnp.where(odd, high, low)


def start_call(diag_inverse, sub_factor, displacement):
    cases, comps, layers, section = displacement.shape
    packed = jax.ShapeDtypeStruct((cases * comps * 3 * section // 128, 128), f32)
    block = pltpu.VMEM((cases, comps, 8, section), f32)
    square = pltpu.VMEM(diag_inverse.shape, f32)
    return pl.pallas_call(
        start_kernel,
        in_specs=[pl.BlockSpec(memory_space=pltpu.HBM)] * 3,
        out_specs=[pl.BlockSpec(memory_space=pltpu.VMEM)] * 3,
        out_shape=[jax.ShapeDtypeStruct(diag_inverse.shape, f32), packed, packed],
        scratch_shapes=[square, square, block, block, pltpu.SemaphoreType.DMA((4,))],
        compiler_params=small(4),
        cost_estimate=pl.CostEstimate(flops=10**10, bytes_accessed=10**6, transcendentals=0),
        name="start",
    )(*in_hbm(diag_inverse, sub_factor, displacement))


def pair_maps_kernel(own_ref, other_ref, maps_ref, mixed_ref):
    order = own_ref.shape[0]
    odd = (lax.axis_index("row") & 1) == 1
    own, other = own_ref[...], other_ref[...]
    first = jnp.where(odd, other, own)
    first_split, second_split = split(first), split(jnp.where(odd, own, other))
    phi = dot3(second_split, first_split, NN)
    phi_split = split(phi)
    gram = dot3(first_split, first_split, TN) + dot3(phi_split, phi_split, TN)
    maps_ref[:order, :] = phi
    maps_ref[order:, :] = gram
    mixed_ref[...] = first + dot3(second_split, phi_split, TN)


def join_maps_kernel(stride, own_ref, other_ref, maps_ref, mixed_ref, half_ref):
    order = own_ref.shape[1]
    upper = (lax.axis_index("row") & stride) != 0
    own, other = own_ref[...], other_ref[...]
    first, second = jnp.where(upper, other, own), jnp.where(upper, own, other)
    first_phi = split(first[:order])
    mixed = dot3(split(second[order:]), first_phi, NN)
    phi = dot3(split(second[:order]), first_phi, NN)
    gram = first[order:] + dot3(first_phi, split(mixed), TN)
    maps_ref[:order, :] = phi
    maps_ref[order:, :] = gram
    mixed_ref[...] = mixed
    odd = (lax.axis_index("row") & 1) == 1
    half_ref[...] = jnp.where(odd, gram, phi)


def maps_call(kernel, name, extra, own, other):
    order = own.shape[1]
    return pl.pallas_call(
        kernel,
        out_shape=[
            jax.ShapeDtypeStruct((2 * order, order), f32),
        ]
        + [jax.ShapeDtypeStruct((order, order), f32)] * extra,
        compiler_params=small(3),
        cost_estimate=pl.CostEstimate(flops=10**10, bytes_accessed=10**6, transcendentals=0),
        name=name,
    )(own, other)


def pair_shifts_kernel(own_ref, other_ref, own_step_ref, other_step_ref, maps_ref, mixed_ref, out_ref):
    cases, order = own_ref.shape
    odd = (lax.axis_index("row") & 1) == 1
    own, other = own_ref[...], other_ref[...]
    first, second = jnp.where(odd, other, own), jnp.where(odd, own, other)
    second_step = jnp.where(odd, own_step_ref[...], other_step_ref[...])
    out_ref[:cases, :] = dot_rows(first, split(second_step), NT) + second
    out_ref[cases:, :] = -(
        dot_rows(first, split(mixed_ref[...]), NN)
        + dot_rows(second, split(maps_ref[:order, :]), NN)
    )


def join_shifts_kernel(stride, own_ref, other_ref, own_maps_ref, other_maps_ref, mixed_ref, out_ref):
    order = mixed_ref.shape[0]
    cases = own_ref.shape[0] // 2
    upper = (lax.axis_index("row") & stride) != 0
    own, other = own_ref[...], other_ref[...]
    first, second = jnp.where(upper, other, own), jnp.where(upper, own, other)
    own_phi, other_phi = own_maps_ref[:order, :], other_maps_ref[:order, :]
    first_phi = jnp.where(upper, other_phi, own_phi)
    second_phi = jnp.where(upper, own_phi, other_phi)
    out_ref[:cases, :] = dot_rows(first[:cases], split(second_phi), NT) + second[:cases]
    out_ref[cases:, :] = (
        first[cases:]
        + dot_rows(second[cases:], split(first_phi), NN)
        - dot_rows(first[:cases], split(mixed_ref[...]), NN)
    )


def shifts_call(kernel, name, cases, *operands):
    return pl.pallas_call(
        kernel,
        out_shape=jax.ShapeDtypeStruct((2 * cases, operands[0].shape[1]), f32),
        compiler_params=small(3),
        name=name,
    )(*operands)


def local_kernel(strides, *refs):
    levels = []
    for stride in strides:
        levels.append((stride, *refs[:4]))
        refs = refs[4:]
    (own_step_ref, other_step_ref, own_value_ref, other_value_ref, inverse_ref, from_ahead_ref,
     from_back_ref, rest_ref) = refs
    cases, order = own_value_ref.shape
    mine = lax.axis_index("row")
    odd = (mine & 1) == 1
    eye = (
        lax.broadcasted_iota(jnp.int32, (order, order), 0)
        == lax.broadcasted_iota(jnp.int32, (order, order), 1)
    ).astype(f32)
    none, last = jnp.zeros((order, order), f32), jnp.zeros((cases, order), f32)
    ahead = jnp.concatenate([eye, none, last], axis=0)
    back = jnp.concatenate([none, eye, last], axis=0)

    def shifted(value):
        return jnp.concatenate([none, none, value], axis=0)

    for stride, own_maps, other_maps, own_shifts, other_shifts in levels[::-1]:
        upper = (mine & stride) != 0
        first_phi = jnp.where(upper, other_maps[:order, :], own_maps[:order, :])
        second_maps = jnp.where(upper, own_maps[...], other_maps[...])
        own, other = own_shifts[...], other_shifts[...]
        first_shift = jnp.where(upper, other[:cases], own[:cases])
        second_shift = jnp.where(upper, own[cases:], other[cases:])
        middle = dot_rows(ahead, split(first_phi), NT) + shifted(first_shift)
        inner = (
            dot_rows(back, split(second_maps[:order]), NN)
            - dot_rows(middle, split(second_maps[order:]), NN)
            + shifted(second_shift)
        )
        ahead = jnp.where(upper, middle, ahead)
        back = jnp.where(upper, back, inner)

    own_step, other_step = own_step_ref[...], other_step_ref[...]
    own_value, other_value = own_value_ref[...], other_value_ref[...]
    first_step = split(jnp.where(odd, other_step, own_step))
    second_step = split(jnp.where(odd, own_step, other_step))
    first = dot_rows(ahead, first_step, NT) + shifted(jnp.where(odd, other_value, own_value))
    second = dot_rows(first, second_step, NT) + shifted(jnp.where(odd, own_value, other_value))
    inner = dot_rows(back - second, second_step, NN)
    solved = dot_rows(
        jnp.where(odd, second - back, first - inner), split(inverse_ref[...]), NN
    )
    from_ahead_ref[...] = solved[:order]
    from_back_ref[...] = solved[order : 2 * order]
    rest_ref[...] = solved[2 * order :]


def local_call(strides, levels, leaf):
    order = leaf[0].shape[0]
    cases = leaf[2].shape[0]
    square = jax.ShapeDtypeStruct((order, order), f32)
    return pl.pallas_call(
        functools.partial(local_kernel, strides),
        out_shape=[square, square, jax.ShapeDtypeStruct((cases, order), f32)],
        compiler_params=small(6),
        cost_estimate=pl.CostEstimate(flops=10**9, bytes_accessed=10**6, transcendentals=0),
        name="local_solution",
    )(*levels, *leaf)


def finish_kernel(width, ways, *refs):
    own_maps_ref, got_ref, swapped_ref, *refs = refs
    order = own_maps_ref.shape[1]
    shifts, refs = refs[:ways], refs[ways:]
    (from_ahead_ref, from_back_ref, rest_ref, inner_base, outer_base,
     labels_ref,
     weight_ref, updated_hbm, solution_hbm, all_maps, all_shifts, ahead_ref, back_ref, updated,
     solution, out_sems) = refs
    cases = rest_ref.shape[0]
    comps, layers, section = labels_ref.shape
    mine = lax.axis_index("row")
    odd = (mine & 1) == 1
    group = mine // width

    all_maps[group] = own_maps_ref[...]
    for hop in range(1, ways):
        part = slice((hop - 1) * order, hop * order)
        got, swapped = got_ref[part, :], swapped_ref[part, :]
        all_maps[group ^ hop, :order] = jnp.where(odd, got, swapped)
        all_maps[group ^ hop, order:] = jnp.where(odd, swapped, got)
    for hop in range(ways):
        all_shifts[group ^ hop_order[hop]] = shifts[hop][...]

    ahead = all_shifts[0, :cases]
    ahead_ref[0] = jnp.zeros_like(ahead)
    ahead_ref[1] = ahead
    for at in range(1, ways - 1):
        ahead = dot_rows(ahead, split(all_maps[at, :order]), NT) + all_shifts[at, :cases]
        ahead_ref[at + 1] = ahead
    back = jnp.zeros_like(ahead)
    back_ref[ways - 1] = back
    for at in range(ways - 1, 0, -1):
        own = all_shifts[at, cases:] - dot_rows(ahead_ref[at], split(all_maps[at, order:]), NN)
        last = at == ways - 1
        back = own if last else own + dot_rows(back, split(all_maps[at, :order]), NN)
        back_ref[at - 1] = back
    ahead, back = ahead_ref[group], back_ref[group]

    solved = (
        dot_rows(ahead, split(from_ahead_ref[...]), NN)
        + dot_rows(back, split(from_back_ref[...]), NN)
        + rest_ref[...]
    )
    solution[...] = solved
    out_copies = [pltpu.make_async_copy(solution, solution_hbm, out_sems.at[comps])]
    out_copies[0].start()

    for comp in range(comps):
        for tile in range(section // 128):
            lanes = slice(tile * 128, (tile + 1) * 128)
            label = labels_ref[comp, :, lanes]
            weight = weight_ref[comp, :, lanes]
            for case in range(cases):
                table = jnp.broadcast_to(solved[case : case + 1, :], (layers, 128))
                spread = jnp.take_along_axis(table, label, axis=1, mode="promise_in_bounds")
                correction = weight * spread
                middle = slice(8, layers - 8)
                updated[case, comp, middle, lanes] = (
                    inner_base[case, comp, :, lanes] + correction[8 : layers - 8]
                )
                updated[case, comp, :8, lanes] = outer_base[case, comp, :8, lanes] + correction[:8]
                updated[case, comp, layers - 8 :, lanes] = (
                    outer_base[case, comp, 8:, lanes] + correction[layers - 8 :]
                )
        copy = pltpu.make_async_copy(
            updated.at[:, comp], updated_hbm.at[:, comp], out_sems.at[comp]
        )
        copy.start()
        out_copies.append(copy)
    for copy in out_copies:
        copy.wait()


def finish_call(width, maps, shifts, local_maps, inner, outer, labels, weight):
    cases, comps, _, section = inner.shape
    layers = labels.shape[1]
    whole = (cases, comps, layers, section)
    order = maps[0].shape[1]
    ways = len(shifts)
    hbm, local = pl.BlockSpec(memory_space=pltpu.HBM), pl.BlockSpec(memory_space=pltpu.VMEM)
    before = (*maps, *[shifts[hop] for hop in hop_order], *local_maps)
    return pl.pallas_call(
        functools.partial(finish_kernel, width, ways),
        in_specs=[local] * (len(before) + 4),
        out_specs=[hbm, hbm],
        out_shape=[
            jax.ShapeDtypeStruct(whole, f32),
            jax.ShapeDtypeStruct((cases, order), f32),
        ],
        scratch_shapes=[
            pltpu.VMEM((ways, 2 * order, order), f32),
            pltpu.VMEM((ways, 2 * cases, order), f32),
            pltpu.VMEM((ways, cases, order), f32),
            pltpu.VMEM((ways, cases, order), f32),
            pltpu.VMEM(whole, f32),
            pltpu.VMEM((cases, order), f32),
            pltpu.SemaphoreType.DMA((comps + 1,)),
        ],
        compiler_params=small(10),
        name="finish",
    )(*before, inner, outer, labels, weight)


def per_device(
    displacement, loads, section_stiffness, modulus, aggregate, basis_weight, diag_inverse, sub_factor
):
    count = lax.axis_size("row")
    ways = 4
    width = count // ways

    def swap(value, mask):
        return lax.ppermute(value, "row", [(i, i ^ mask) for i in range(count)])

    step, near, far = start_call(diag_inverse, sub_factor, displacement)
    other_step = swap(step, 1)
    near = swap(near, 1)
    far = lax.ppermute(
        far, "row", [(i, i + 1 if i & 1 else i - 1) for i in range(1, count - 1)]
    )
    cases, comps, layers, section = displacement.shape
    order = diag_inverse.shape[0]
    outer = (comps, cases, 16, section)
    node_values = (modulus, aggregate, basis_weight)
    inner_base, outer_across, diagonal, total = residual_call(
        inner_kernel,
        False,
        [
            (cases, comps, layers - 16, section),
            outer,
            (comps, 8, section),
            (4 * cases, order // 2),
        ],
        [pltpu.VMEM((comps, cases, layers - 16, section), f32)],
        displacement, loads, section_stiffness, *node_values,
    )
    maps, mixed = maps_call(pair_maps_kernel, "pair_maps", 1, step, other_step)
    pair_operands = (step, other_step, maps, mixed)
    strides, joins = [], []
    stride = 2
    while stride < width:
        other_maps = swap(maps, stride ^ 1)
        if not strides:
            other_maps, total = lax.optimization_barrier((other_maps, total))
        joined, mixed, half = maps_call(
            functools.partial(join_maps_kernel, stride), "join_maps", 2, maps, other_maps
        )
        strides.append(stride)
        joins.append((maps, other_maps, mixed))
        maps = joined
        stride *= 2
    def needed(source, target):
        block = source // width
        return target // width < block if source & 1 else 0 < block < ways - 1

    halves = []
    for hop in range(1, ways):
        moves = [(i, i ^ (hop * width ^ 1)) for i in range(count)]
        halves.append(lax.ppermute(half, "row", [move for move in moves if needed(*move)]))
    outer_base, value = residual_call(
        outer_kernel,
        True,
        [(cases, comps, 16, section), (cases, order)],
        [],
        displacement, loads, *node_values, diag_inverse, near, far, outer_across, diagonal, total,
    )
    other_value = swap(value, 1)
    shifts = shifts_call(pair_shifts_kernel, "pair_shifts", cases, value, other_value, *pair_operands)
    levels = []
    for stride, (own_maps, other_maps, mixed) in zip(strides, joins):
        other_shifts = swap(shifts, stride ^ 1)
        levels += [own_maps, other_maps, shifts, other_shifts]
        shifts = shifts_call(
            functools.partial(join_shifts_kernel, stride), "join_shifts", cases,
            shifts, other_shifts, own_maps, other_maps, mixed,
        )
    gathered = jnp.concatenate(lax.optimization_barrier((shifts, *halves))[1:], axis=0)
    all_maps = [maps, gathered, swap(gathered, 1)]
    all_shifts = [shifts] + [swap(shifts, hop * width ^ 1) for hop in range(1, ways)]
    leaf = (step, other_step, value, other_value, diag_inverse)
    local_maps = local_call(tuple(strides), levels, leaf)
    updated, solution_rows = finish_call(
        width, all_maps, all_shifts, local_maps, inner_base, outer_base, aggregate, basis_weight
    )
    return updated, solution_rows.T


def solution(mesh):
    placed = (
        P("groups", None, "row", None),
        P("groups", None, "row", None),
        P("groups", None, None),
        P("row", "groups"),
        P("groups", "row", None),
        P("groups", "row", None),
        P("row", "groups"),
        P("row", "groups"),
    )
    return jax.shard_map(
        per_device,
        mesh=mesh,
        in_specs=placed,
        out_specs=(P("groups", None, "row", None), P("row", "groups")),
        check_vma=False,
    )
```
